32 devices in a mesh: ctx: 8 (over y, x, core), exp: 4 (over z).
Axes of the slice: x: 2, y: 2, z: 4, core: 2. Of those that a mesh axis runs over, the one named last changes fastest.
Arguments:
- lin_query: bfloat16 [1024, 8192], P('ctx', 'exp'), may hold values from -5 to 5
- lin_key: bfloat16 [1024, 8192], P('ctx', 'exp'), may hold values from -5 to 5
- lin_value: bfloat16 [1024, 8192], P('ctx', 'exp'), may hold values from -5 to 5
- log_decay: float32 [1024, 64], P('ctx', 'exp'), may hold values from -1.5 to 0
- lin_gain: float32 [8192], P('exp'), may hold values from 0.25 to 1.75
- moe_input: bfloat16 [192, 6144], P(('ctx', 'exp')), may hold values from -6 to 6
- routes: int32 [192, 2], P(('ctx', 'exp')), may hold values from 0 to 7, all different within a row; in each aligned block of 6 rows (0 to 5, 6 to 11, ...) at most 2 rows name the same one
- route_weight: float32 [192, 2], P(('ctx', 'exp')), may hold values from 0.2 to 1
- gate_weight: bfloat16 [8, 6144, 9216], P('exp', None, 'ctx'), may hold values from -0.078125 to 0.078125
- up_weight: bfloat16 [8, 6144, 9216], P('exp', None, 'ctx'), may hold values from -0.078125 to 0.078125
- down_weight: bfloat16 [8, 9216, 6144], P('exp', 'ctx'), may hold values from -0.0625 to 0.0625
- soft_query: bfloat16 [1024, 8192], P('ctx', 'exp'), may hold values from -5 to 5
- soft_kv: bfloat16 [1024, 8, 2, 128], P('ctx', 'exp'), may hold values from -5 to 5
Outputs:
- lin_out: bfloat16 [1024, 8192], P('ctx', 'exp')
- moe_out: bfloat16 [192, 6144], P(('ctx', 'exp'))
- soft_out: bfloat16 [1024, 8192], P('ctx', 'exp')
The draws below stay inside these ranges and needn't reach their ends.
Inputs may be any that keep to these rules, and one draw needn't show every extreme that they name: `routes`: within the rows of one device (6 rows) each expert is named by at most 2 of them; the 2 experts of a row differ.
All inputs are finite; a program needn't handle non-finite values.
Results may differ from the reference program's by a relative error of at most 0.009.
Values may be sent and summed in bfloat16 or wider, within the bound.
No kernel may reach another device: no remote copies, remote signals or barrier semaphores. Data moves between devices by JAX's collectives and lax.ppermute only.
A program may use at most 192 MiB of HBM per device.

```python
import math
import jax
import jax.numpy as jnp
import numpy as np
from jax import lax

D = 6144
HEAD_TOTAL = 64
HEAD = 128
KV_HEADS = 8
FF = 9216
EXPERTS = 8
TOP = 2
SEQ_DEV = 128
MOE_DEV = 6
CAP = 2
CONTEXT_LENGTH = 1024
MOE_TOKENS = 192


def draw_log_decay(key, part):
    random_subkeys = jax.random.split(key, 6)
    fast_cut = 5
    fast_head = jax.random.randint(random_subkeys[0], (HEAD_TOTAL,), 0, 10) < fast_cut
    fast_rate = jax.random.uniform(random_subkeys[1], (HEAD_TOTAL,), jnp.float32, 0.05, 0.1)
    slow_rate = jax.random.uniform(random_subkeys[2], (HEAD_TOTAL,), jnp.float32, 0.1, 0.4) / CONTEXT_LENGTH
    head_rate = jnp.where(fast_head, fast_rate, slow_rate)
    region_span = max(CONTEXT_LENGTH // 16, 1)
    token_positions = jnp.arange(CONTEXT_LENGTH)
    region = jnp.minimum(token_positions // region_span, 15)
    region_factor = jnp.exp(jax.random.uniform(random_subkeys[3], (16,), jnp.float32, -0.7, 0.7))
    step_fraction = region_factor[region][:, None] * head_rate[None, :]
    spike_locations = jax.random.randint(random_subkeys[4], (2,), 0, CONTEXT_LENGTH)
    spike_losses = jnp.log(jax.random.uniform(random_subkeys[5], (2, HEAD_TOTAL), jnp.float32, 0.55, 0.8))
    spike_events = jnp.zeros((CONTEXT_LENGTH, HEAD_TOTAL), jnp.float32)
    for item_count in range(2):
        spike_events = spike_events + jnp.where((token_positions == spike_locations[item_count])[:, None], spike_losses[item_count][None, :], 0.0)
    return (spike_events - step_fraction).astype(jnp.float32)


def draw_soft_query(key, part):
    base_key = jax.random.fold_in(key, 1)
    values = jnp.clip(jax.random.normal(base_key, (CONTEXT_LENGTH, HEAD_TOTAL * HEAD), jnp.float32), -4.0, 4.0)
    return values.astype(jnp.bfloat16)


def draw_soft_kv(key, part):
    base_key = jax.random.fold_in(key, 2)
    values = jnp.clip(jax.random.normal(base_key, (CONTEXT_LENGTH, KV_HEADS, 2, HEAD), jnp.float32), -4.0, 4.0)
    return values.astype(jnp.bfloat16)


def steps_of(rng, shape, cuts, low, top_value):
    level, own = 1.0, jax.random.fold_in(rng, 6)
    for dim, blocks in cuts:
        heights = jnp.exp(jax.random.uniform(jax.random.fold_in(own, dim), (blocks,), jnp.float32, low / len(cuts), top_value / len(cuts)))
        level = level * jnp.repeat(heights, shape[dim] // blocks).reshape([-1 if axis == dim else 1 for axis in range(len(shape))])
    return level


def shared_out(rng, own, number, rows, count, top, most, slope):
    order = jax.random.permutation(rng, count)
    packed, ordinary = portions_of(count, rows * top, most, slope, True), portions_of(count, rows * top, most, slope, False)
    places = jnp.arange(count)

    def named(tallies, offset_by):
        used = int((tallies > 0).sum())
        fixed = max(1, used // 4)
        passed = fixed + (places - fixed + offset_by * (used - fixed)) % max(1, count - fixed)
        return jnp.zeros((count,), jnp.int32).at[order[jnp.where(places < fixed, places, passed)]].set(jnp.asarray(tallies, jnp.int32))

    tallies = jnp.where(number % 4 == 0, named(packed, number // 4), named(ordinary, number - number // 4 - 1))
    mixed = jax.random.permutation(jax.random.fold_in(own, 3), count)
    donor, taker = mixed[0:count // 2 * 2:2], mixed[1:count // 2 * 2:2]
    margin = jnp.minimum(tallies[donor] - 1, most - tallies[taker]) // 2
    margin = jnp.where((donor == order[0]) | (taker == order[0]) | (tallies[taker] == 0), 0, jnp.maximum(margin, 0))
    passed = jax.random.randint(jax.random.fold_in(own, 4), (count // 2,), 0, 1 << 20) % (margin + 1)
    tallies = tallies.at[donor].add(-passed).at[taker].add(passed)
    members = jnp.searchsorted(jnp.cumsum(tallies), jnp.arange(rows * top), side="right").astype(jnp.int32)
    grid = members.reshape(top, rows).T
    grid = grid[jax.random.permutation(jax.random.fold_in(own, 1), rows)]
    offset_by = jax.random.randint(jax.random.fold_in(own, 2), (rows, 1), 0, top)
    return jnp.take_along_axis(grid, (jnp.arange(top)[None, :] + offset_by) % top, axis=1)


def portions_of(amount, total, limit, lean, full):
    weights = [(1 << 20) // math.isqrt(standing ** lean) + 1 for standing in range(1, amount + 1)]
    largest = limit if full else min(limit, max(-(-total // amount), total * weights[0] // sum(weights)))
    least = 1 if total - largest >= amount - 1 else 0
    holding, rest = [largest] + [least] * (amount - 1), total - largest - least * (amount - 1)
    while rest > 0:
        candidates = [i for i in range(1, amount) if holding[i] < largest] or [i for i in range(1, amount) if holding[i] < limit]
        whole, left = sum([weights[i] for i in candidates]), rest
        for i in candidates:
            addition = min(limit - holding[i], max(1, left * weights[i] // whole), rest)
            holding[i] = holding[i] + addition
            rest = rest - addition
    return np.array(holding)


def gaussian(rng, shape, scale, bound, cuts=(), held_as=jnp.bfloat16):
    drawn = scale * jax.random.normal(rng, shape, jnp.float32)
    if cuts:
        drawn = drawn * steps_of(rng, shape, cuts, -0.22, 0.18)
    return jnp.clip(drawn, -bound, bound).astype(held_as)


def setup_inputs(seed: int = 0) -> dict:
    key_list = jax.random.split(jax.random.key(seed), 14)
    lin_query = gaussian(key_list[0], (CONTEXT_LENGTH, HEAD_TOTAL * HEAD), 1.0, 5.0, ((0, 8), (1, 4)))
    lin_key = gaussian(key_list[1], (CONTEXT_LENGTH, HEAD_TOTAL * HEAD), 1.0, 5.0, ((0, 8), (1, 4)))
    lin_value = gaussian(key_list[2], (CONTEXT_LENGTH, HEAD_TOTAL * HEAD), 1.0, 5.0, ((0, 8), (1, 4)))
    log_decay = draw_log_decay(jax.random.fold_in(key_list[13], 71), 0)
    lin_gain = jnp.clip(1.0 + 0.15 * jax.random.normal(key_list[4], (HEAD_TOTAL * HEAD,), jnp.float32), 0.25, 1.75)
    moe_input = gaussian(key_list[5], (MOE_TOKENS, D), 1.0, 6.0, ((0, 32),))
    routes_keys = jax.random.split(jax.random.fold_in(key_list[6], 1), MOE_TOKENS // MOE_DEV)
    routes_turns = jax.random.permutation(jax.random.fold_in(key_list[6], 3), MOE_TOKENS // MOE_DEV)
    routes = jax.vmap(lambda own, number: shared_out(jax.random.fold_in(key_list[6], 2), own, number, MOE_DEV, EXPERTS, TOP, CAP, 1))(routes_keys, routes_turns).reshape((MOE_TOKENS, TOP))
    route_weight = jnp.clip(0.2 + 0.8 * jax.random.uniform(key_list[7], (MOE_TOKENS, TOP), jnp.float32) ** steps_of(key_list[7], (MOE_TOKENS, TOP), ((0, 32),), -0.2, 0.2), 0.2, 1.0)
    gate_weight = gaussian(key_list[8], (EXPERTS, D, FF), D ** -0.5, 0.078125, ((0, 4), (2, 8)))
    up_weight = gaussian(key_list[9], (EXPERTS, D, FF), D ** -0.5, 0.078125, ((0, 4), (2, 8)))
    down_weight = gaussian(key_list[10], (EXPERTS, FF, D), FF ** -0.5, 0.0625, ((0, 4), (1, 8)))
    soft_query = draw_soft_query(jax.random.fold_in(key_list[13], 71), 0)
    soft_kv = draw_soft_kv(jax.random.fold_in(key_list[13], 71), 0)
    return {"lin_query": lin_query, "lin_key": lin_key, "lin_value": lin_value, "log_decay": log_decay, "lin_gain": lin_gain, "moe_input": moe_input, "routes": routes, "route_weight": route_weight, "gate_weight": gate_weight, "up_weight": up_weight, "down_weight": down_weight, "soft_query": soft_query, "soft_kv": soft_kv}


def lightning_ref(lin_query, lin_key, lin_value, log_decay, lin_gain):
    block_count = CONTEXT_LENGTH // SEQ_DEV
    score_scale = 1.0 / math.sqrt(HEAD)
    query_blocks = lin_query.reshape(block_count, SEQ_DEV, HEAD_TOTAL, HEAD)
    key_blocks = lin_key.reshape(block_count, SEQ_DEV, HEAD_TOTAL, HEAD)
    value_blocks = lin_value.reshape(block_count, SEQ_DEV, HEAD_TOTAL, HEAD)
    decay_blocks = log_decay.reshape(block_count, SEQ_DEV, HEAD_TOTAL)
    causal = jnp.tril(jnp.ones((SEQ_DEV, SEQ_DEV), dtype=jnp.bool_))

    def block_step(running_state, inputs):
        query_part, key_part, value_part, decay_part = inputs
        query_f = query_part.astype(jnp.float32)
        key_f = key_part.astype(jnp.float32)
        value_f = value_part.astype(jnp.float32)
        cumulative = jnp.cumsum(decay_part, axis=0)
        scores = jnp.einsum('thd,jhd->htj', query_f, key_f, precision=lax.Precision.HIGHEST) * score_scale
        spread = cumulative.T[:, :, None] - cumulative.T[:, None, :]
        decays = jnp.where(causal[None], jnp.exp(jnp.where(causal[None], spread, 0.0)), 0.0)
        within = jnp.einsum('htj,jhd->thd', scores * decays, value_f, precision=lax.Precision.HIGHEST)
        carried = jnp.exp(cumulative)[:, :, None] * jnp.einsum('thd,hde->the', query_f, running_state, precision=lax.Precision.HIGHEST) * score_scale
        tail_decay = jnp.exp(cumulative[-1][None, :] - cumulative)
        local_state = jnp.einsum('th,thd,the->hde', tail_decay, key_f, value_f, precision=lax.Precision.HIGHEST)
        next_state = jnp.exp(cumulative[-1])[:, None, None] * running_state + local_state
        return (next_state, within + carried)
    start_state = jnp.zeros((HEAD_TOTAL, HEAD, HEAD), jnp.float32)
    final_state, combined = lax.scan(block_step, start_state, (query_blocks, key_blocks, value_blocks, decay_blocks))
    combined = combined.reshape(CONTEXT_LENGTH, HEAD_TOTAL, HEAD)
    root_mean = jnp.sqrt(lax.optimization_barrier(jnp.mean(combined * combined, axis=-1, keepdims=True)) + 1e-06)
    normed = combined / root_mean * lin_gain.reshape(HEAD_TOTAL, HEAD)
    return normed.reshape(CONTEXT_LENGTH, HEAD_TOTAL * HEAD).astype(jnp.bfloat16)

def experts_ref(moe_input, routes, route_weight, gate_weight, up_weight, down_weight):
    block_count = MOE_TOKENS // MOE_DEV
    pair_count = MOE_DEV * TOP
    flat_ids = routes.reshape(block_count, pair_count)
    same_expert = flat_ids[:, :, None] == flat_ids[:, None, :]
    pair_order = jnp.arange(pair_count, dtype=jnp.int32)
    earlier_pair = pair_order[None, :] < pair_order[:, None]
    slot_rank = lax.optimization_barrier(jnp.sum(jnp.logical_and(same_expert, earlier_pair[None]), axis=2)).astype(jnp.int32)
    block_ids = jnp.arange(block_count, dtype=jnp.int32)[:, None]
    row_index = (block_ids * CAP + slot_rank).astype(jnp.int32)
    pair_rows = jnp.repeat(moe_input, TOP, axis=0).reshape(block_count, pair_count, D)
    buffer = jnp.zeros((EXPERTS, block_count * CAP, D), jnp.bfloat16).at[flat_ids, row_index].set(pair_rows)

    def expert(inputs):
        tokens_in, gate_w, up_w, down_w = inputs
        gate_part = jnp.dot(tokens_in, gate_w, preferred_element_type=jnp.float32)
        up_part = jnp.dot(tokens_in, up_w, preferred_element_type=jnp.float32)
        hidden = (jax.nn.silu(gate_part) * up_part).astype(jnp.bfloat16)
        return jnp.dot(hidden, down_w, preferred_element_type=jnp.float32).astype(jnp.bfloat16)
    results = lax.map(expert, (buffer, gate_weight, up_weight, down_weight))
    pair_out = results[flat_ids, row_index].reshape(MOE_TOKENS, TOP, D).astype(jnp.float32)
    mixed = lax.optimization_barrier(jnp.sum(pair_out * route_weight[:, :, None], axis=1))
    return mixed.astype(jnp.bfloat16)

def softmax_ref(soft_query, soft_kv):
    group = HEAD_TOTAL // KV_HEADS
    score_scale = 1.0 / math.sqrt(HEAD)
    queries = soft_query.reshape(CONTEXT_LENGTH, HEAD_TOTAL, HEAD).transpose(1, 0, 2)
    keys_all = jnp.repeat(soft_kv[:, :, 0, :].transpose(1, 0, 2), group, axis=0)
    values_all = jnp.repeat(soft_kv[:, :, 1, :].transpose(1, 0, 2), group, axis=0)
    causal = jnp.tril(jnp.ones((CONTEXT_LENGTH, CONTEXT_LENGTH), dtype=jnp.bool_))

    def one_head(inputs):
        query_head, key_head, value_head = inputs
        scores = jnp.dot(query_head, key_head.T, preferred_element_type=jnp.float32) * score_scale
        scores = jnp.where(causal, scores, -jnp.inf)
        weights = jax.nn.softmax(scores, axis=-1).astype(jnp.bfloat16)
        return jnp.dot(weights, value_head, preferred_element_type=jnp.float32).astype(jnp.bfloat16)
    outputs = lax.map(one_head, (queries, keys_all, values_all))
    return outputs.transpose(1, 0, 2).reshape(CONTEXT_LENGTH, HEAD_TOTAL * HEAD)

def reference(lin_query, lin_key, lin_value, log_decay, lin_gain, moe_input, routes, route_weight, gate_weight, up_weight, down_weight, soft_query, soft_kv):
    lin_out = lightning_ref(lin_query, lin_key, lin_value, log_decay, lin_gain)
    moe_out = experts_ref(moe_input, routes, route_weight, gate_weight, up_weight, down_weight)
    soft_out = softmax_ref(soft_query, soft_kv)
    return (lin_out, moe_out, soft_out)
```

```python
import functools
import math

import jax
import jax.numpy as jnp
from jax import lax
from jax.experimental import pallas as pl
from jax.experimental.pallas import tpu as pltpu
from jax.sharding import PartitionSpec as P

TOP = 2
CAP = 2
F32 = jnp.float32
BF16 = jnp.bfloat16
MASKED = -1e30


vmem_spec = pl.BlockSpec(memory_space=pltpu.VMEM)
smem_spec = pl.BlockSpec(memory_space=pltpu.SMEM)
any_spec = pl.BlockSpec(memory_space=pl.ANY)


def shape(dims, dtype):
    return jax.ShapeDtypeStruct(tuple(dims), dtype)


def params(mib):
    return pltpu.CompilerParams(vmem_limit_bytes=mib << 20)


def cost(flops, nbytes):
    return pl.CostEstimate(flops=flops, bytes_accessed=nbytes, transcendentals=0)


def swap(value, axis, bit):
    count = lax.axis_size(axis)
    return lax.ppermute(value, axis, [(i, i ^ (1 << bit)) for i in range(count)])


def order_of(bits):
    found = [0]
    for bit in bits:
        found = found + [one ^ (1 << bit) for one in found]
    return found


def slot_matrix(routes_ref, rows, experts, slots, weight_ref=None):
    named = [[routes_ref[r, k] for k in range(TOP)] for r in range(rows)]
    flat = [one for row in named for one in row]
    at_slot = lax.broadcasted_iota(jnp.int32, (slots, rows), 0)
    at_row = lax.broadcasted_iota(jnp.int32, (slots, rows), 1)
    matrix = jnp.zeros((slots, rows), F32)
    for i, mine in enumerate(flat):
        rank = jnp.int32(0)
        for other in flat[:i]:
            rank = rank + (other == mine).astype(jnp.int32)
        slot = mine * CAP + rank
        value = 1.0 if weight_ref is None else weight_ref[i // TOP, i % TOP]
        matrix = matrix + jnp.where((at_slot == slot) & (at_row == i // TOP), value, 0.0)
    return matrix


def pack(moe_input, routes, experts):
    rows, width = moe_input.shape
    slots = experts * CAP

    def kernel(routes_ref, x_ref, out_ref):
        matrix = slot_matrix(routes_ref, rows, experts, slots).astype(BF16)
        out_ref[...] = jnp.dot(matrix, x_ref[...], preferred_element_type=F32).astype(BF16)

    return pl.pallas_call(
        kernel,
        in_specs=[smem_spec, vmem_spec],
        out_specs=vmem_spec,
        out_shape=shape((slots, width), BF16),
        compiler_params=params(4),
    )(routes, moe_input)


def unpack(returned, routes, route_weight):
    slots, width = returned.shape
    rows = routes.shape[0]

    def kernel(routes_ref, weight_ref, y_ref, out_ref):
        matrix = slot_matrix(routes_ref, rows, slots // CAP, slots, weight_ref)
        out_ref[...] = lax.dot_general(
            matrix,
            y_ref[...].astype(F32),
            (((0,), (0,)), ((), ())),
            precision=lax.Precision.HIGHEST,
            preferred_element_type=F32,
        ).astype(BF16)

    return pl.pallas_call(
        kernel,
        in_specs=[smem_spec, smem_spec, vmem_spec],
        out_specs=vmem_spec,
        out_shape=shape((rows, width), BF16),
        compiler_params=params(4),
    )(routes, route_weight, returned)


def divisor(total, most, unit=128):
    return max(d for d in range(unit, most + 1, unit) if total % d == 0)


def experts_kernel(near, far, gate_weight, up_weight, down_weight):
    half, width = near.shape
    rows = 2 * half
    experts, _, hidden = gate_weight.shape
    deep = divisor(width, 1024)
    wide = divisor(width, 768)
    first, second = width // deep, width // wide
    steps = experts * first
    slots, later = min(3, steps), min(3, second)

    def kernel(near_ref, far_ref, gate_ref, up_ref, down_ref, keep_ref, send_ref,
               x_ref, gates, ups, downs, gate_sum, up_sum, inner, sems, down_sems):
        def fetch(i):
            e, s, slot = lax.div(i, first), lax.rem(i, first), lax.rem(i, slots)
            at = pl.ds(pl.multiple_of(s * deep, deep), deep)
            return (
                pltpu.make_async_copy(gate_ref.at[e, at], gates.at[slot], sems.at[0, slot]),
                pltpu.make_async_copy(up_ref.at[e, at], ups.at[slot], sems.at[1, slot]),
            )

        def fetch_down(i):
            slot = lax.rem(i, later)
            at = pl.ds(pl.multiple_of(i * wide, 128), wide)
            return [
                pltpu.make_async_copy(down_ref.at[e, :, at], downs.at[slot, e], down_sems.at[slot, e])
                for e in range(experts)
            ]

        for i in range(slots):
            for copy in fetch(i):
                copy.start()
        x_ref[:half] = near_ref[...]
        x_ref[half:] = far_ref[...]
        expert_of = lax.rem(
            lax.div(lax.broadcasted_iota(jnp.int32, (rows, hidden), 0), CAP), experts
        )

        def upward(i, carry):
            e, s, slot = lax.div(i, first), lax.rem(i, first), lax.rem(i, slots)
            for copy in fetch(i):
                copy.wait()
            x = x_ref[:, pl.ds(pl.multiple_of(s * deep, 128), deep)]
            gate = jnp.dot(x, gates[slot], preferred_element_type=F32)
            up = jnp.dot(x, ups[slot], preferred_element_type=F32)

            @pl.when(s == 0)
            def _():
                gate_sum[...] = gate
                up_sum[...] = up

            @pl.when(s > 0)
            def _():
                gate_sum[...] += gate
                up_sum[...] += up

            @pl.when(i + slots < steps)
            def _():
                for copy in fetch(i + slots):
                    copy.start()

            @pl.when((i + slots >= steps) & (i + slots - steps < later))
            def _():
                for copy in fetch_down(i + slots - steps):
                    copy.start()

            @pl.when(s == first - 1)
            def _():
                gated = gate_sum[...]
                value = gated / (1.0 + jnp.exp(-gated)) * up_sum[...]
                inner[e] = jnp.where(expert_of == e, value, 0.0).astype(BF16)

            return carry

        lax.fori_loop(0, steps, upward, 0)
        for i in range(slots, later):
            for copy in fetch_down(i):
                copy.start()

        def downward(i, carry):
            slot = lax.rem(i, later)
            for copy in fetch_down(i):
                copy.wait()
            total = jnp.dot(inner[0], downs[slot, 0], preferred_element_type=F32)
            for e in range(1, experts):
                total = total + jnp.dot(inner[e], downs[slot, e], preferred_element_type=F32)
            at = pl.ds(pl.multiple_of(i * wide, 128), wide)
            keep_ref[:, at] = total[:half]
            send_ref[:, at] = total[half:].astype(BF16)

            @pl.when(i + later < second)
            def _():
                for copy in fetch_down(i + later):
                    copy.start()

            return carry

        lax.fori_loop(0, second, downward, 0)

    return pl.pallas_call(
        kernel,
        in_specs=[vmem_spec, vmem_spec, any_spec, any_spec, any_spec],
        out_specs=[vmem_spec, vmem_spec],
        out_shape=[shape((half, width), F32), shape((half, width), BF16)],
        scratch_shapes=[
            pltpu.VMEM((rows, width), BF16),
            pltpu.VMEM((slots, deep, hidden), BF16),
            pltpu.VMEM((slots, deep, hidden), BF16),
            pltpu.VMEM((later, experts, hidden, wide), BF16),
            pltpu.VMEM((rows, hidden), F32),
            pltpu.VMEM((rows, hidden), F32),
            pltpu.VMEM((experts, rows, hidden), BF16),
            pltpu.SemaphoreType.DMA((2, slots)),
            pltpu.SemaphoreType.DMA((later, experts)),
        ],
        compiler_params=params(56),
        cost_estimate=cost(
            6 * rows * experts * width * hidden, 6 * experts * width * hidden
        ),
    )(near, far, gate_weight, up_weight, down_weight)


def join(left, right, left_order, right_order, block):
    rows, part = left.shape

    def kernel(left_ref, right_ref, out_ref):
        out_ref[:, :part] = left_ref[...]
        for to, one in enumerate(left_order):
            at = right_order.index(one) * block
            out_ref[to * block : (to + 1) * block, part:] = right_ref[at : at + block]

    return pl.pallas_call(
        kernel,
        in_specs=[vmem_spec] * 2,
        out_specs=vmem_spec,
        out_shape=shape((rows, 2 * part), BF16),
        compiler_params=params(8),
    )(left, right)


def fold_first(keep, got, left_order, right_order, block):
    rows, width = keep.shape
    part, half = width // 2, rows // 2

    def kernel(keep_ref, got_ref, lk, ls, rk, rs):
        for to, one in enumerate(left_order):
            at = slice(to * block, (to + 1) * block)
            value = keep_ref[at, :part] + got_ref[at, :part].astype(F32)
            if to * block < half:
                lk[at] = value
            else:
                ls[to * block - half : (to + 1) * block - half] = value.astype(BF16)
        for to, one in enumerate(right_order):
            source = left_order.index(one)
            at = slice(source * block, (source + 1) * block)
            value = keep_ref[at, part:] + got_ref[at, part:].astype(F32)
            if to * block < half:
                rk[to * block : (to + 1) * block] = value
            else:
                rs[to * block - half : (to + 1) * block - half] = value.astype(BF16)

    return pl.pallas_call(
        kernel,
        in_specs=[vmem_spec] * 2,
        out_specs=[vmem_spec] * 4,
        out_shape=[shape((half, part), F32), shape((half, part), BF16)] * 2,
        compiler_params=params(16),
    )(keep, got)


def fold(lk, lg, rk, rg):
    rows, part = lk.shape
    half = rows // 2

    def kernel(lk_ref, lg_ref, rk_ref, rg_ref, lko, lso, rko, rso):
        for keep, got, out, send in ((lk_ref, lg_ref, lko, lso), (rk_ref, rg_ref, rko, rso)):
            out[...] = keep[:half] + got[:half].astype(F32)
            send[...] = (keep[half:] + got[half:].astype(F32)).astype(BF16)

    return pl.pallas_call(
        kernel,
        in_specs=[vmem_spec] * 4,
        out_specs=[vmem_spec] * 4,
        out_shape=[shape((half, part), F32), shape((half, part), BF16)] * 2,
        compiler_params=params(16),
    )(lk, lg, rk, rg)


def fold_last(lk, lg, rk, rg):
    rows, part = lk.shape

    def kernel(lk_ref, lg_ref, rk_ref, rg_ref, out_ref):
        out_ref[:, :part] = (lk_ref[...] + lg_ref[...].astype(F32)).astype(BF16)
        out_ref[:, part:] = (rk_ref[...] + rg_ref[...].astype(F32)).astype(BF16)

    return pl.pallas_call(
        kernel,
        in_specs=[vmem_spec] * 4,
        out_specs=vmem_spec,
        out_shape=shape((rows, 2 * part), BF16),
        compiler_params=params(8),
    )(lk, lg, rk, rg)


EXTRA = 8


def sums_of(decay_ref):
    length = decay_ref.shape[0]
    row = lax.broadcasted_iota(jnp.int32, (length, length), 0)
    column = lax.broadcasted_iota(jnp.int32, (length, length), 1)
    lower = (column <= row).astype(F32)
    upper = (row <= column).astype(F32)
    down = jnp.dot(
        lower, decay_ref[...], precision=lax.Precision.HIGHEST, preferred_element_type=F32
    )
    across = lax.dot_general(
        decay_ref[...],
        upper,
        (((0,), (0,)), ((), ())),
        precision=lax.Precision.HIGHEST,
        preferred_element_type=F32,
    )
    return down, across


def put_message(ref, j, state, factor):
    size = state.shape[0]
    ref[j, :size] = state.astype(BF16)
    coarse = factor.astype(BF16)
    fine = (factor - coarse.astype(F32)).astype(BF16)
    which = lax.broadcasted_iota(jnp.int32, (EXTRA, state.shape[1]), 0)
    ref[j, size:] = jnp.where(
        which == 0, coarse.astype(F32), jnp.where(which == 1, fine.astype(F32), 0.0)
    ).astype(BF16)


def get_message(ref, j):
    size = ref.shape[1] - EXTRA
    state = ref[j, :size].astype(F32)
    tail = ref[j, size:].astype(F32)
    return state, tail[0:1] + tail[1:2]


def local_states(parity, lin_key, lin_value, log_decay):
    length, heads = log_decay.shape
    size = lin_key.shape[1] // heads
    half = heads // 2

    def kernel(parity_ref, key_ref, value_ref, decay_ref, mine_ref, factor_ref, send_ref):
        down, _ = sums_of(decay_ref)
        step = pl.program_id(0)
        second = (parity_ref[0] ^ step) == 1
        down = jnp.where(second, down[:, half:], down[:, :half])
        last = down[length - 1 : length]
        tail = jnp.exp(last - down)
        factor = jnp.exp(last)
        for j in range(half):
            at = slice(j * size, (j + 1) * size)
            keyed = (key_ref[:, at].astype(F32) * tail[:, j : j + 1]).astype(BF16)
            state = lax.dot_general(
                keyed, value_ref[:, at], (((0,), (0,)), ((), ())), preferred_element_type=F32
            )
            whole = jnp.broadcast_to(factor[:, j : j + 1], (1, size))

            @pl.when(step == 0)
            def _():
                mine_ref[j] = state
                factor_ref[j : j + 1] = whole

            @pl.when(step == 1)
            def _():
                put_message(send_ref, j, state, whole)

    block = pl.BlockSpec((length, half * size), lambda i, p: (0, p[0] ^ i))
    full = lambda dims: pl.BlockSpec(dims, lambda i, p: (0,) * len(dims))
    return pl.pallas_call(
        kernel,
        grid_spec=pltpu.PrefetchScalarGridSpec(
            num_scalar_prefetch=1,
            grid=(2,),
            in_specs=[block, block, full((length, heads))],
            out_specs=[
                full((half, size, size)),
                full((half, size)),
                full((half, size + EXTRA, size)),
            ],
        ),
        out_shape=[
            shape((half, size, size), F32),
            shape((half, size), F32),
            shape((half, size + EXTRA, size), BF16),
        ],
        compiler_params=params(8),
        cost_estimate=cost(4 * heads * length * size * size, 4 * length * heads * size),
    )(parity, lin_key, lin_value, log_decay)


def join_pair(parity, mine, factor, got):
    half, size, _ = mine.shape

    def kernel(parity_ref, mine_ref, factor_ref, got_ref, sum_ref, sum_factor_ref, send_ref):
        odd = parity_ref[0] == 1
        for j in range(half):
            own, own_factor = mine_ref[j], factor_ref[j : j + 1]
            other, other_factor = get_message(got_ref, j)
            total = jnp.where(odd, own + own_factor * other, other + other_factor * own)
            both = own_factor * other_factor
            sum_ref[j] = total
            sum_factor_ref[j : j + 1] = both
            put_message(send_ref, j, total, both)

    return pl.pallas_call(
        kernel,
        in_specs=[smem_spec] + [vmem_spec] * 3,
        out_specs=[vmem_spec] * 3,
        out_shape=[
            shape((half, size, size), F32),
            shape((half, size), F32),
            shape((half, size + EXTRA, size), BF16),
        ],
        compiler_params=params(8),
    )(parity, mine, factor, got)


def join_group(upper, total, factor, before, before_factor, got):
    half, size, _ = total.shape
    first = before is None
    earlier = () if first else (before, before_factor)

    def kernel(upper_ref, total_ref, factor_ref, got_ref, *refs):
        if first:
            sum_ref, sum_factor_ref, send_ref, before_out, before_factor_out = refs
        else:
            (before_ref, before_factor_ref,
             sum_ref, sum_factor_ref, send_ref, before_out, before_factor_out) = refs
        high = upper_ref[0] == 1
        for j in range(half):
            own, own_factor = total_ref[j], factor_ref[j : j + 1]
            other, other_factor = get_message(got_ref, j)
            if first:
                prior, prior_factor = jnp.zeros_like(own), jnp.ones_like(own_factor)
            else:
                prior, prior_factor = before_ref[j], before_factor_ref[j : j + 1]
            before_out[j] = jnp.where(high, prior + prior_factor * other, prior)
            before_factor_out[j : j + 1] = jnp.where(
                high, prior_factor * other_factor, prior_factor
            )
            joined = jnp.where(high, own + own_factor * other, other + other_factor * own)
            both = own_factor * other_factor
            sum_ref[j] = joined
            sum_factor_ref[j : j + 1] = both
            put_message(send_ref, j, joined, both)

    return pl.pallas_call(
        kernel,
        in_specs=[smem_spec] + [vmem_spec] * (3 + len(earlier)),
        out_specs=[vmem_spec] * 5,
        out_shape=[
            shape((half, size, size), F32),
            shape((half, size), F32),
            shape((half, size + EXTRA, size), BF16),
            shape((half, size, size), F32),
            shape((half, size), F32),
        ],
        compiler_params=params(12),
    )(upper, total, factor, got, *earlier)


def join_end(flags, before, before_factor, got, mine, factor, neighbour):
    half, size, _ = mine.shape
    given = [one for one in (before, before_factor, got) if one is not None]

    def kernel(flags_ref, *refs):
        refs = list(refs)
        before_ref = refs.pop(0) if before is not None else None
        before_factor_ref = refs.pop(0) if before is not None else None
        got_ref = refs.pop(0) if got is not None else None
        mine_ref, factor_ref, neighbour_ref, keep_ref, send_ref = refs
        high, odd = flags_ref[0] == 1, flags_ref[1] == 1
        for j in range(half):
            state = jnp.zeros((size, size), F32)
            if before_ref is not None:
                state = before_ref[j]
            if got_ref is not None:
                other, _ = get_message(got_ref, j)
                scaled = other if before_ref is None else before_factor_ref[j : j + 1] * other
                state = jnp.where(high, state + scaled, state)
            other, other_factor = get_message(neighbour_ref, j)
            even_state = jnp.where(odd, other, mine_ref[j])
            even_factor = jnp.where(odd, other_factor, factor_ref[j : j + 1])
            for_odd = even_state + even_factor * state
            keep_ref[j] = jnp.where(odd, for_odd, state).astype(BF16)
            send_ref[j] = jnp.where(odd, state, for_odd).astype(BF16)

    return pl.pallas_call(
        kernel,
        in_specs=[smem_spec] + [vmem_spec] * (len(given) + 3),
        out_specs=[vmem_spec] * 2,
        out_shape=[shape((half, size, size), BF16)] * 2,
        compiler_params=params(8),
    )(flags, *given, mine, factor, neighbour)


def lightning(parity, lin_query, lin_key, lin_value, log_decay, lin_gain, near, far):
    length, heads = log_decay.shape
    size = lin_key.shape[1] // heads
    half = heads // 2
    scale = 1.0 / math.sqrt(size)

    def kernel(parity_ref, query_ref, key_ref, value_ref, decay_ref, gain_ref, near_ref, far_ref,
               out_ref):
        down, across = sums_of(decay_ref)
        step = pl.program_id(0)
        second = (parity_ref[0] ^ step) == 1
        down = jnp.where(second, down[:, half:], down[:, :half])
        across = jnp.where(second, across[half:], across[:half])
        risen = jnp.exp(down) * scale
        row = lax.broadcasted_iota(jnp.int32, (length, length), 0)
        column = lax.broadcasted_iota(jnp.int32, (length, length), 1)
        causal = column <= row
        for j in range(half):
            at = slice(j * size, (j + 1) * size)
            query, key, value = query_ref[:, at], key_ref[:, at], value_ref[:, at]
            scores = lax.dot_general(
                query, key, (((1,), (1,)), ((), ())), preferred_element_type=F32
            )
            spread = down[:, j : j + 1] - across[j : j + 1]
            decays = jnp.exp(jnp.where(causal, spread, MASKED))
            mixed = (scores * (decays * scale)).astype(BF16)
            prior = jnp.where(step == 0, near_ref[j], far_ref[j])
            combined = jnp.dot(mixed, value, preferred_element_type=F32)
            combined = combined + risen[:, j : j + 1] * jnp.dot(
                query, prior, preferred_element_type=F32
            )
            square = jnp.mean(combined * combined, axis=-1, keepdims=True) + 1e-06
            out_ref[:, at] = (combined * lax.rsqrt(square) * gain_ref[:, at]).astype(BF16)

    block = pl.BlockSpec((length, half * size), lambda i, p: (0, p[0] ^ i))
    gains = pl.BlockSpec((1, half * size), lambda i, p: (0, p[0] ^ i))
    full = lambda dims: pl.BlockSpec(dims, lambda i, p: (0,) * len(dims))
    return pl.pallas_call(
        kernel,
        grid_spec=pltpu.PrefetchScalarGridSpec(
            num_scalar_prefetch=1,
            grid=(2,),
            in_specs=[
                block, block, block, full((length, heads)), gains,
                full((half, size, size)), full((half, size, size)),
            ],
            out_specs=block,
        ),
        out_shape=shape(lin_query.shape, BF16),
        compiler_params=params(12),
        cost_estimate=cost(6 * heads * length * size * size, 8 * length * heads * size),
    )(parity, lin_query, lin_key, lin_value, log_decay, lin_gain.reshape(1, -1), near, far)


def softmax_layer(index, soft_query, pieces, order, groups, size):
    length, width = soft_query.shape
    heads = width // size // groups
    total = sum(one.shape[0] for one in pieces)
    scale = 1.0 / math.sqrt(size)

    def kernel(index_ref, query_ref, *refs):
        piece_refs, out_ref = refs[: len(pieces)], refs[len(pieces)]
        keys, values, bias = refs[len(pieces) + 1 :]
        group = pl.program_id(0)
        at = 0
        for one in piece_refs:
            count = one.shape[0]
            keys[at : at + count] = one[:, :size]
            values[at : at + count] = one[:, size:]
            at += count

        @pl.when(group == 0)
        def _():
            me = index_ref[0]
            row = lax.broadcasted_iota(jnp.int32, (length, length), 0)
            column = lax.broadcasted_iota(jnp.int32, (length, length), 1)
            own = jnp.where(column <= row, 0.0, MASKED)
            for j, one in enumerate(order):
                if one == 0:
                    part = own
                else:
                    part = jnp.full((length, length), jnp.where((me ^ one) < me, 0.0, MASKED))
                bias[:, j * length : (j + 1) * length] = part

        for h in range(heads):
            at = slice(h * size, (h + 1) * size)
            scores = lax.dot_general(
                query_ref[:, at], keys[...], (((1,), (1,)), ((), ())), preferred_element_type=F32
            )
            scores = scores * scale + bias[...]
            weights = jnp.exp(scores - jnp.max(scores, axis=-1, keepdims=True))
            summed = jnp.sum(weights, axis=-1, keepdims=True)
            mixed = jnp.dot(weights.astype(BF16), values[...], preferred_element_type=F32)
            out_ref[:, at] = (mixed / summed).astype(BF16)

    block = pl.BlockSpec((length, heads * size), lambda g: (0, g))
    return pl.pallas_call(
        kernel,
        grid=(groups,),
        in_specs=[smem_spec, block]
        + [pl.BlockSpec((one.shape[0], 2 * size), lambda g: (0, g)) for one in pieces],
        out_specs=block,
        out_shape=shape(soft_query.shape, BF16),
        scratch_shapes=[
            pltpu.VMEM((total, size), BF16),
            pltpu.VMEM((total, size), BF16),
            pltpu.VMEM((length, total), F32),
        ],
        compiler_params=params(24),
        cost_estimate=cost(4 * width * length * total, 4 * length * width),
    )(index, soft_query, *pieces)


def on_device(
    lin_query, lin_key, lin_value, log_decay, lin_gain,
    moe_input, routes, route_weight, gate_weight, up_weight, down_weight,
    soft_query, soft_kv,
):
    count, planes = lax.axis_size("ctx"), lax.axis_size("exp")
    me = lax.axis_index("ctx").astype(jnp.int32)
    bits = list(range(count.bit_length() - 1))
    high = bits[1:]
    left_bits, right_bits = high, high[::-1]
    bit_of = lambda b: ((me >> b) & 1).reshape(1)
    parity = bit_of(0)
    experts_here = gate_weight.shape[0]
    experts = experts_here * planes
    width = moe_input.shape[1]
    part = width // 2

    outgoing = pack(moe_input, routes, experts).reshape(planes, experts_here * CAP, width)
    arrived = lax.all_to_all(outgoing, "exp", split_axis=0, concat_axis=0, tiled=True)
    block = planes * experts_here * CAP
    arrived = arrived.reshape(block, width)
    left, right = arrived[:, :part], arrived[:, part:]
    for lb, rb in zip(left_bits, right_bits):
        left_got, right_got = swap(left, "ctx", lb), swap(right, "ctx", rb)
        left = jnp.concatenate([left, left_got])
        right = jnp.concatenate([right, right_got])
    left_order, right_order = order_of(left_bits), order_of(right_bits)
    near = join(left, right, left_order, right_order, block)
    far = swap(near, "ctx", 0)

    mine, factor, message = local_states(parity, lin_key, lin_value, log_decay)
    neighbour = swap(message, "ctx", 0)
    before = before_factor = got = None
    if high:
        total, total_factor, message = join_pair(parity, mine, factor, neighbour)
        for b in high:
            got = swap(message, "ctx", b)
            if b != high[-1]:
                total, total_factor, message, before, before_factor = join_group(
                    bit_of(b), total, total_factor, before, before_factor, got
                )
    flags = jnp.concatenate([bit_of(high[-1] if high else 0), parity])
    state_near, state_send = join_end(flags, before, before_factor, got, mine, factor, neighbour)
    state_far = swap(state_send, "ctx", 0)

    groups, size = soft_kv.shape[1], soft_kv.shape[3]
    held = soft_kv.reshape(soft_kv.shape[0], groups * 2 * size)
    pieces = [held]
    for b in high + [0]:
        held = pieces[0] if len(pieces) == 1 else jnp.concatenate(pieces)
        pieces = [held, swap(held, "ctx", b)]

    keep, send = experts_kernel(near, far, gate_weight, up_weight, down_weight)

    got = swap(send, "ctx", 0)
    lk, ls, rk, rs = fold_first(keep, got, left_order, right_order, block)
    for i in reversed(range(len(high))):
        lg, rg = swap(ls, "ctx", left_bits[i]), swap(rs, "ctx", right_bits[i])
        if i:
            lk, ls, rk, rs = fold(lk, lg, rk, rg)
    result = fold_last(lk, lg, rk, rg).reshape(planes, experts_here * CAP, width)
    returned = lax.all_to_all(result, "exp", split_axis=0, concat_axis=0, tiled=True)
    moe_out = unpack(returned.reshape(block, width), routes, route_weight)

    soft_out = softmax_layer(
        me.reshape(1), soft_query, pieces, order_of(high + [0]), groups, size
    )
    lin_out = lightning(
        parity, lin_query, lin_key, lin_value, log_decay, lin_gain, state_near, state_far
    )
    return (lin_out, moe_out, soft_out)


def solution(mesh):
    placed = (
        P("ctx", "exp"),
        P("ctx", "exp"),
        P("ctx", "exp"),
        P("ctx", "exp"),
        P("exp"),
        P(("ctx", "exp"), None),
        P(("ctx", "exp"), None),
        P(("ctx", "exp"), None),
        P("exp", None, "ctx"),
        P("exp", None, "ctx"),
        P("exp", "ctx", None),
        P("ctx", "exp"),
        P("ctx", "exp", None, None),
    )
    return jax.shard_map(
        on_device,
        mesh=mesh,
        in_specs=placed,
        out_specs=(P("ctx", "exp"), P(("ctx", "exp"), None), P("ctx", "exp")),
        check_vma=False,
    )
```

```python
import functools
import math

import jax
import jax.numpy as jnp
from jax import lax
from jax.experimental import pallas as pl
from jax.experimental.pallas import tpu as pltpu
from jax.sharding import PartitionSpec as P


TOP = 2
CAP = 2
F32 = jnp.float32
BF16 = jnp.bfloat16
MASKED = -1e30


vmem_spec = pl.BlockSpec(memory_space=pltpu.VMEM)
smem_spec = pl.BlockSpec(memory_space=pltpu.SMEM)
any_spec = pl.BlockSpec(memory_space=pl.ANY)
hbm_spec = pl.BlockSpec(memory_space=pltpu.HBM)


def shape(dims, dtype):
    return jax.ShapeDtypeStruct(tuple(dims), dtype)


def params(mib):
    return pltpu.CompilerParams(vmem_limit_bytes=mib << 20)


def cost(flops, nbytes):
    return pl.CostEstimate(flops=flops, bytes_accessed=nbytes, transcendentals=0)


def swap(value, axis, offset):
    return lax.ppermute(value, axis, [(i, i ^ offset) for i in range(lax.axis_size(axis))])


def tie(*values):
    return lax.optimization_barrier(values)


def in_hbm(*values):
    return [pltpu.with_memory_space_constraint(one, pltpu.HBM) for one in values]


def slot_matrix(flags_ref, routes_ref, rows, slots, here, weight_ref=None):
    named = [[routes_ref[k, r] for k in range(TOP)] for r in range(rows)]
    flat = [one for row in named for one in row]
    at_slot = lax.broadcasted_iota(jnp.int32, (slots, rows), 0)
    at_row = lax.broadcasted_iota(jnp.int32, (slots, rows), 1)
    matrix = jnp.zeros((slots, rows), F32)
    for i, mine in enumerate(flat):
        rank = jnp.int32(0)
        for other in flat[:i]:
            rank = rank + (other == mine).astype(jnp.int32)
        place = (lax.div(mine, here) ^ flags_ref[2]) * here + lax.rem(mine, here)
        slot = place * CAP + rank
        value = 1.0 if weight_ref is None else weight_ref[i % TOP, i // TOP]
        matrix = matrix + jnp.where((at_slot == slot) & (at_row == i // TOP), value, 0.0)
    return matrix


def pack(flags, moe_input, routes, planes, experts):
    rows, width = moe_input.shape
    slots = experts * CAP
    part = width // 2
    each = slots // planes

    def kernel(flags_ref, routes_ref, x_ref, *out_refs):
        matrix = slot_matrix(flags_ref, routes_ref, rows, slots, experts // planes)
        matrix = matrix.astype(BF16)
        for h in range(2):
            at = pl.ds(pl.multiple_of((flags_ref[1] ^ h) * part, 128), part)
            value = jnp.dot(matrix, x_ref[:, at], preferred_element_type=F32)
            for p, out_ref in enumerate(out_refs):
                out_ref[:, h * part : (h + 1) * part] = value[p * each : (p + 1) * each].astype(BF16)

    return pl.pallas_call(
        kernel,
        in_specs=[smem_spec, smem_spec, vmem_spec],
        out_specs=[vmem_spec] * planes,
        out_shape=[shape((each, width), BF16)] * planes,
        compiler_params=params(2),
    )(flags, routes.T, *in_hbm(moe_input))


def arrange(arrived):
    each, width = arrived[0].shape
    part = width // 2

    def kernel(*refs):
        *in_refs, own_ref, other_ref = refs
        for h, out_ref in enumerate((own_ref, other_ref)):
            at = slice(h * part, (h + 1) * part)
            out_ref[...] = jnp.concatenate([one[:, at].astype(F32) for one in in_refs]).astype(BF16)

    return pl.pallas_call(
        kernel,
        in_specs=[vmem_spec] * len(arrived),
        out_specs=[vmem_spec] * 2,
        out_shape=[shape((len(arrived) * each, part), BF16)] * 2,
        compiler_params=params(2),
    )(*arrived)


def unpack(flags, returned, routes, route_weight):
    planes = len(returned)
    each, width = returned[0].shape
    slots = planes * each
    rows = routes.shape[0]
    part = width // 2

    def kernel(flags_ref, routes_ref, weight_ref, *refs):
        *y_refs, out_ref = refs
        matrix = slot_matrix(flags_ref, routes_ref, rows, slots, each // CAP, weight_ref)
        pieces = []
        for _ in range(3):
            pieces.append(matrix.astype(BF16))
            matrix = matrix - pieces[-1].astype(F32)
        for h in range(2):
            y = jnp.concatenate(
                [one[:, h * part : (h + 1) * part].astype(F32) for one in y_refs]
            ).astype(BF16)
            total = None
            for piece in pieces:
                term = lax.dot_general(
                    piece, y, (((0,), (0,)), ((), ())), preferred_element_type=F32
                )
                total = term if total is None else total + term
            at = pl.ds(pl.multiple_of((flags_ref[1] ^ h) * part, 128), part)
            out_ref[:, at] = total.astype(BF16)

    return pl.pallas_call(
        kernel,
        in_specs=[smem_spec] * 3 + [vmem_spec] * planes,
        out_specs=vmem_spec,
        out_shape=shape((rows, width), BF16),
        compiler_params=params(4),
    )(flags, routes.T, route_weight.T, *returned)


def divisor(total, most, unit=128):
    return max(d for d in range(unit, most + 1, unit) if total % d == 0)


def gate_and_up(flags, which, x_half, gate_half, up_weight, sums=None, down_weight=None):
    rows, part = x_half.shape
    experts, _, hidden = gate_half.shape
    deep = divisor(part, 1536)
    chunks = part // deep
    final = sums is not None
    given = 1 if final else 0
    left = max(1, experts - given)
    ahead = columns_ahead(part)
    blocks = lax.axis_size("ctx")
    block = rows // blocks

    def kernel(flags_ref, x_ref, gate_ref, up_ref, *refs):
        if final:
            (gate_in, up_in, up_first, down_ref, inner_ref, early_ref,
             ups, sems, early_sems, x_held) = refs
        else:
            gate_out, up_out, next_ref, ups, sems, next_sem = refs
        half = flags_ref[1] ^ which

        def fetch(e, s):
            at = pl.ds(pl.multiple_of(half * part + s * deep, deep), deep)
            return pltpu.make_async_copy(up_ref.at[e, at], ups.at[e - given, s], sems.at[e - given, s])

        for e in range(given, experts):
            for s in range(chunks):
                fetch(e, s).start()
        if not final:
            rest = pl.ds(pl.multiple_of((1 - half) * part, part), part)
            following = pltpu.make_async_copy(up_ref.at[0, rest], next_ref, next_sem)
            following.start()
        if final:
            early = fetch_ahead(flags_ref[1] ^ 1, part, ahead, down_ref, early_ref, early_sems)
            for copy in early:
                copy.start()
            expert_of = lax.rem(
                lax.div(lax.broadcasted_iota(jnp.int32, (rows, 1), 0), CAP), experts
            )
        if final:
            for k in range(blocks):
                x_held[k * block : (k + 1) * block] = x_ref[(k ^ 1) * block : ((k ^ 1) + 1) * block]
            x_ref = x_held
        for e in range(experts):
            gate = jnp.dot(x_ref[...], gate_ref[e], preferred_element_type=F32)
            if final:
                gate_in[e] = gate_in[e] + gate
            else:
                gate_out[e] = gate
            if e < given:
                weight = up_first[...]
            else:
                for s in range(chunks):
                    fetch(e, s).wait()
                weight = ups[e - given].reshape(part, hidden)
            up = jnp.dot(x_ref[...], weight, preferred_element_type=F32)
            if final:
                gated = gate_in[e]
                value = gated / (1.0 + jnp.exp(-gated)) * (up_in[e] + up)
                here = jnp.broadcast_to(expert_of, (rows, hidden)) == e
                inner_ref[e] = jnp.where(here, value, 0.0).astype(BF16)
            else:
                up_out[e] = up
        if final:
            for copy in early:
                copy.wait()
        else:
            following.wait()

    partial = shape((experts, rows, hidden), F32)
    scratch = [
        pltpu.VMEM((left, chunks, deep, hidden), BF16),
        pltpu.SemaphoreType.DMA((left, chunks)),
    ]
    if final:
        out_shape = [
            pltpu.VMEM((experts, rows, hidden), BF16),
            pltpu.VMEM((experts, hidden, ahead), BF16),
        ]
        scratch = scratch + [
            pltpu.SemaphoreType.DMA((experts,)), pltpu.VMEM((rows, part), BF16)
        ]
        operands, specs = (*sums, *in_hbm(down_weight)), [vmem_spec] * 3 + [hbm_spec]
    else:
        out_shape = [partial, partial, pltpu.VMEM((part, hidden), BF16)]
        scratch = scratch + [pltpu.SemaphoreType.DMA]
        operands, specs = (), []
    return pl.pallas_call(
        kernel,
        in_specs=[smem_spec, vmem_spec, vmem_spec, hbm_spec] + specs,
        out_specs=[vmem_spec] * len(out_shape),
        out_shape=out_shape,
        scratch_shapes=scratch,
        compiler_params=params(18),
        cost_estimate=cost(4 * rows * experts * part * hidden, 4 * experts * part * hidden),
    )(flags, x_half, gate_half, *in_hbm(up_weight), *operands)


def down_step(part):
    return divisor(part, 1024)


def columns_ahead(part):
    wide = down_step(part)
    return max(1, (part // wide) * 2 // 3) * wide


def fetch_ahead(half, part, ahead, weight_ref, to_ref, sems):
    at = pl.ds(pl.multiple_of(half * part, 128), ahead)
    return [
        pltpu.make_async_copy(weight_ref.at[e, :, at], to_ref.at[e], sems.at[e])
        for e in range(to_ref.shape[0])
    ]


def down(flags, which, inner, early, down_weight):
    experts, rows, hidden = inner.shape
    part = down_weight.shape[2] // 2
    wide = down_step(part)
    ahead = early.shape[2]
    done = ahead // wide
    steps = part // wide
    left = max(1, steps - done)
    block = rows // lax.axis_size("ctx")

    def kernel(flags_ref, inner_ref, early_ref, down_ref, out_ref, *refs):
        if which == 1:
            next_ref, downs, sems, next_sems = refs
        else:
            downs, sems = refs
        half = flags_ref[1] ^ which

        def fetch(i):
            at = pl.ds(pl.multiple_of(half * part + i * wide, 128), wide)
            return [
                pltpu.make_async_copy(
                    down_ref.at[e, :, at], downs.at[i - done, e], sems.at[i - done, e]
                )
                for e in range(experts)
            ]

        for i in range(done, steps):
            for copy in fetch(i):
                copy.start()
        if which == 1:
            following = fetch_ahead(flags_ref[1], part, ahead, down_ref, next_ref, next_sems)
            for copy in following:
                copy.start()
        for i in range(steps):
            if i >= done:
                for copy in fetch(i):
                    copy.wait()
            total = None
            for e in range(experts):
                weight = early_ref[e, :, i * wide : (i + 1) * wide] if i < done else downs[i - done, e]
                term = jnp.dot(inner_ref[e], weight, preferred_element_type=F32)
                total = term if total is None else total + term
            at = slice(i * wide, (i + 1) * wide)
            if which == 0:
                out_ref[:, at] = total
            else:
                for k in range(rows // block):
                    out_ref[k * block : (k + 1) * block, at] = total[
                        (k ^ 1) * block : ((k ^ 1) + 1) * block
                    ].astype(BF16)
        if which == 1:
            for copy in following:
                copy.wait()

    scratch = [
        pltpu.VMEM((left, experts, hidden, wide), BF16),
        pltpu.SemaphoreType.DMA((left, experts)),
    ]
    out_shape = [shape((rows, part), BF16 if which == 1 else F32)]
    if which == 1:
        out_shape.append(pltpu.VMEM((experts, hidden, ahead), BF16))
        scratch.append(pltpu.SemaphoreType.DMA((experts,)))
    return pl.pallas_call(
        kernel,
        in_specs=[smem_spec, vmem_spec, vmem_spec, hbm_spec],
        out_specs=[vmem_spec] * len(out_shape),
        out_shape=out_shape,
        scratch_shapes=scratch,
        compiler_params=params(12),
        cost_estimate=cost(rows * experts * 2 * part * hidden, 2 * experts * part * hidden),
    )(flags, inner, early, *in_hbm(down_weight))


def fold_pair(keep, got, pieces):
    rows, part = keep.shape
    each = rows // pieces

    def kernel(keep_ref, got_ref, out_ref, *send_refs):
        out_ref[...] = keep_ref[:each] + got_ref[:each].astype(F32)
        for k, send_ref in enumerate(send_refs, 1):
            at = slice(k * each, (k + 1) * each)
            send_ref[...] = (keep_ref[at] + got_ref[at].astype(F32)).astype(BF16)

    return pl.pallas_call(
        kernel,
        in_specs=[vmem_spec] * 2,
        out_specs=[vmem_spec] * pieces,
        out_shape=[shape((each, part), F32)] + [shape((each, part), BF16)] * (pieces - 1),
        compiler_params=params(4),
    )(keep, got)


def fold_all(keep, got):
    rows, part = keep.shape
    half = rows // 2

    def kernel(keep_ref, *refs):
        *got_refs, out_ref, send_ref = refs
        total = keep_ref[...]
        for one in got_refs:
            total = total + one[...].astype(F32)
        out_ref[...] = total[:half].astype(BF16)
        send_ref[...] = total[half:].astype(BF16)

    return pl.pallas_call(
        kernel,
        in_specs=[vmem_spec] * (1 + len(got)),
        out_specs=[vmem_spec] * 2,
        out_shape=[shape((half, part), BF16)] * 2,
        compiler_params=params(4),
    )(keep, *got)


def finish(own, other, planes):
    rows, part = own.shape
    each = rows // planes

    def kernel(own_ref, other_ref, *out_refs):
        for h, ref in enumerate((own_ref, other_ref)):
            value = ref[...].astype(F32)
            for p, out_ref in enumerate(out_refs):
                out_ref[:, h * part : (h + 1) * part] = value[p * each : (p + 1) * each].astype(BF16)

    return pl.pallas_call(
        kernel,
        in_specs=[vmem_spec] * 2,
        out_specs=[vmem_spec] * planes,
        out_shape=[shape((each, 2 * part), BF16)] * planes,
        compiler_params=params(2),
    )(own, other)


EXTRA = 8


def sums_of(decay_ref):
    length = decay_ref.shape[1]
    row = lax.broadcasted_iota(jnp.int32, (length, length), 0)
    column = lax.broadcasted_iota(jnp.int32, (length, length), 1)
    upper = (row <= column).astype(F32)
    across = jnp.dot(
        decay_ref[...], upper, precision=lax.Precision.HIGHEST, preferred_element_type=F32
    )
    return across.T, across


def put_message(ref, j, state, factor):
    size = state.shape[0]
    ref[j, :size] = state.astype(BF16)
    coarse = factor.astype(BF16)
    fine = (factor - coarse.astype(F32)).astype(BF16)
    which = lax.broadcasted_iota(jnp.int32, (EXTRA, state.shape[1]), 0)
    ref[j, size:] = jnp.where(
        which == 0, coarse.astype(F32), jnp.where(which == 1, fine.astype(F32), 0.0)
    ).astype(BF16)


def get_message(ref, j):
    size = ref.shape[1] - EXTRA
    state = ref[j, :size].astype(F32)
    tail = ref[j, size:].astype(F32)
    return state, tail[0:1] + tail[1:2]


def local_states(flags, lin_key, lin_value, log_decay, gate_weight):
    length, heads = log_decay.shape
    size = lin_key.shape[1] // heads
    half = heads // 2
    experts, width, hidden = gate_weight.shape
    part = width // 2
    chunks = 2

    def kernel(flags_ref, key_ref, value_ref, decay_ref, gate_ref, mine_ref, factor_ref, send_ref,
               own_gate, other_gate, sems):
        step = pl.program_id(0)

        def fetch():
            for h, to in enumerate((own_gate, other_gate)):
                for e in range(experts):
                    for c in range(chunks):
                        rows = part // chunks
                        at = pl.ds(
                            pl.multiple_of((flags_ref[1] ^ h) * part + c * rows, rows), rows
                        )
                        yield pltpu.make_async_copy(
                            gate_ref.at[e, at], to.at[e, c * rows : (c + 1) * rows],
                            sems.at[h, e, c],
                        )

        @pl.when(step == 0)
        def _():
            for copy in fetch():
                copy.start()

        down, _ = sums_of(decay_ref)
        second = (flags_ref[1] ^ step) == 1
        down = jnp.where(second, down[:, half:], down[:, :half])
        last = down[length - 1 : length]
        tail = jnp.exp(last - down)
        factor = jnp.exp(last)
        for j in range(half):
            at = slice(j * size, (j + 1) * size)
            keyed = (key_ref[:, at].astype(F32) * tail[:, j : j + 1]).astype(BF16)
            state = lax.dot_general(
                keyed, value_ref[:, at], (((0,), (0,)), ((), ())), preferred_element_type=F32
            )
            whole = jnp.broadcast_to(factor[:, j : j + 1], (1, size))

            @pl.when(step == 0)
            def _():
                mine_ref[j] = state
                factor_ref[j : j + 1] = whole

            @pl.when(step == 1)
            def _():
                put_message(send_ref, j, state, whole)

        @pl.when(step == 1)
        def _():
            for copy in fetch():
                copy.wait()

    block = pl.BlockSpec((length, half * size), lambda i, p: (0, p[1] ^ i))
    full = lambda dims: pl.BlockSpec(dims, lambda i, p: (0,) * len(dims))
    return pl.pallas_call(
        kernel,
        grid_spec=pltpu.PrefetchScalarGridSpec(
            num_scalar_prefetch=1,
            grid=(2,),
            in_specs=[block, block, full((heads, length)), hbm_spec],
            out_specs=[
                full((half, size, size)),
                full((half, size)),
                full((half, size + EXTRA, size)),
                vmem_spec,
                vmem_spec,
            ],
            scratch_shapes=[pltpu.SemaphoreType.DMA((2, experts, chunks))],
        ),
        out_shape=[
            shape((half, size, size), F32),
            shape((half, size), F32),
            shape((half, size + EXTRA, size), BF16),
            pltpu.VMEM((experts, part, hidden), BF16),
            pltpu.VMEM((experts, part, hidden), BF16),
        ],
        compiler_params=params(8),
        cost_estimate=cost(
            4 * heads * length * size * size,
            4 * length * heads * size + 2 * experts * width * hidden,
        ),
    )(flags, *in_hbm(lin_key, lin_value, log_decay.T, gate_weight))


def join_pair(flags, mine, factor, got):
    half, size, _ = mine.shape

    def kernel(flags_ref, mine_ref, factor_ref, got_ref, sum_ref, sum_factor_ref, send_ref):
        odd = flags_ref[1] == 1
        for j in range(half):
            own, own_factor = mine_ref[j], factor_ref[j : j + 1]
            other, other_factor = get_message(got_ref, j)
            total = jnp.where(odd, own + own_factor * other, other + other_factor * own)
            both = own_factor * other_factor
            sum_ref[j] = total
            sum_factor_ref[j : j + 1] = both
            put_message(send_ref, j, total, both)

    return pl.pallas_call(
        kernel,
        in_specs=[smem_spec] + [vmem_spec] * 3,
        out_specs=[vmem_spec] * 3,
        out_shape=[
            shape((half, size, size), F32),
            shape((half, size), F32),
            shape((half, size + EXTRA, size), BF16),
        ],
        compiler_params=params(8),
    )(flags, mine, factor, got)


def join_group(flags, bit, total, factor, before, before_factor, got):
    half, size, _ = total.shape
    first = before is None
    earlier = () if first else (before, before_factor)

    def kernel(flags_ref, total_ref, factor_ref, got_ref, *refs):
        if first:
            sum_ref, sum_factor_ref, send_ref, before_out, before_factor_out = refs
        else:
            (before_ref, before_factor_ref,
             sum_ref, sum_factor_ref, send_ref, before_out, before_factor_out) = refs
        high = ((flags_ref[0] >> bit) & 1) == 1
        for j in range(half):
            own, own_factor = total_ref[j], factor_ref[j : j + 1]
            other, other_factor = get_message(got_ref, j)
            if first:
                prior, prior_factor = jnp.zeros_like(own), jnp.ones_like(own_factor)
            else:
                prior, prior_factor = before_ref[j], before_factor_ref[j : j + 1]
            before_out[j] = jnp.where(high, prior + prior_factor * other, prior)
            before_factor_out[j : j + 1] = jnp.where(
                high, prior_factor * other_factor, prior_factor
            )
            joined = jnp.where(high, own + own_factor * other, other + other_factor * own)
            both = own_factor * other_factor
            sum_ref[j] = joined
            sum_factor_ref[j : j + 1] = both
            put_message(send_ref, j, joined, both)

    return pl.pallas_call(
        kernel,
        in_specs=[smem_spec] + [vmem_spec] * (3 + len(earlier)),
        out_specs=[vmem_spec] * 5,
        out_shape=[
            shape((half, size, size), F32),
            shape((half, size), F32),
            shape((half, size + EXTRA, size), BF16),
            shape((half, size, size), F32),
            shape((half, size), F32),
        ],
        compiler_params=params(12),
    )(flags, total, factor, got, *earlier)


def join_end(flags, bit, before, before_factor, got, mine, factor, neighbour):
    half, size, _ = mine.shape
    given = [one for one in (before, before_factor, got) if one is not None]

    def kernel(flags_ref, *refs):
        refs = list(refs)
        before_ref = refs.pop(0) if before is not None else None
        before_factor_ref = refs.pop(0) if before is not None else None
        got_ref = refs.pop(0) if got is not None else None
        mine_ref, factor_ref, neighbour_ref, keep_ref, send_ref = refs
        high, odd = ((flags_ref[0] >> bit) & 1) == 1, flags_ref[1] == 1
        for j in range(half):
            state = jnp.zeros((size, size), F32)
            if before_ref is not None:
                state = before_ref[j]
            if got_ref is not None:
                other, _ = get_message(got_ref, j)
                scaled = other if before_ref is None else before_factor_ref[j : j + 1] * other
                state = jnp.where(high, state + scaled, state)
            other, other_factor = get_message(neighbour_ref, j)
            even_state = jnp.where(odd, other, mine_ref[j])
            even_factor = jnp.where(odd, other_factor, factor_ref[j : j + 1])
            for_odd = even_state + even_factor * state
            keep_ref[j] = jnp.where(odd, for_odd, state).astype(BF16)
            send_ref[j] = jnp.where(odd, state, for_odd).astype(BF16)

    return pl.pallas_call(
        kernel,
        in_specs=[smem_spec] + [vmem_spec] * (len(given) + 3),
        out_specs=[vmem_spec] * 2,
        out_shape=[shape((half, size, size), BF16)] * 2,
        compiler_params=params(8),
    )(flags, *given, mine, factor, neighbour)


def lightning(flags, lin_query, lin_key, lin_value, log_decay, lin_gain, near, far):
    length, heads = log_decay.shape
    size = lin_key.shape[1] // heads
    half = heads // 2
    scale = 1.0 / math.sqrt(size)

    def kernel(flags_ref, query_ref, key_ref, value_ref, decay_ref, gain_ref, near_ref, far_ref,
               out_ref):
        down, across = sums_of(decay_ref)
        step = pl.program_id(0)
        second = (flags_ref[1] ^ step) == 1
        down = jnp.where(second, down[:, half:], down[:, :half])
        across = jnp.where(second, across[half:], across[:half])
        risen = jnp.exp(down) * scale
        row = lax.broadcasted_iota(jnp.int32, (length, length), 0)
        column = lax.broadcasted_iota(jnp.int32, (length, length), 1)
        causal = column <= row
        for j in range(half):
            at = slice(j * size, (j + 1) * size)
            query, key, value = query_ref[:, at], key_ref[:, at], value_ref[:, at]
            scores = lax.dot_general(
                query, key, (((1,), (1,)), ((), ())), preferred_element_type=F32
            )
            spread = down[:, j : j + 1] - across[j : j + 1]
            decays = jnp.exp(jnp.where(causal, spread, MASKED))
            mixed = (scores * (decays * scale)).astype(BF16)
            prior = jnp.where(step == 0, near_ref[j], far_ref[j])
            combined = jnp.dot(mixed, value, preferred_element_type=F32)
            combined = combined + risen[:, j : j + 1] * jnp.dot(
                query, prior, preferred_element_type=F32
            )
            square = jnp.mean(combined * combined, axis=-1, keepdims=True) + 1e-06
            out_ref[:, at] = (combined * lax.rsqrt(square) * gain_ref[:, at]).astype(BF16)

    block = pl.BlockSpec((length, half * size), lambda i, p: (0, p[1] ^ i))
    gains = pl.BlockSpec((1, half * size), lambda i, p: (0, p[1] ^ i))
    full = lambda dims: pl.BlockSpec(dims, lambda i, p: (0,) * len(dims))
    return pl.pallas_call(
        kernel,
        grid_spec=pltpu.PrefetchScalarGridSpec(
            num_scalar_prefetch=1,
            grid=(2,),
            in_specs=[
                block, block, block, full((heads, length)), gains,
                full((half, size, size)), full((half, size, size)),
            ],
            out_specs=block,
        ),
        out_shape=shape(lin_query.shape, BF16),
        compiler_params=params(12),
        cost_estimate=cost(6 * heads * length * size * size, 8 * length * heads * size),
    )(flags, lin_query, lin_key, lin_value, log_decay.T, lin_gain.reshape(1, -1), near, far)


def softmax_layer(flags, which, soft_query, pieces, turn, groups, size, heads, so_far=None):
    length, _ = soft_query.shape
    total = sum(one.shape[0] for one in pieces)
    scale = math.log2(math.e) / math.sqrt(size)
    given = () if so_far is None else (so_far,)

    def kernel(flags_ref, query_ref, *refs):
        piece_refs = refs[: len(pieces)]
        out_ref, keys, values, bias = refs[len(pieces) + len(given) :]
        at = 0
        for one in piece_refs:
            count = one.shape[0]
            keys[at : at + count] = one[:, :size]
            values[at : at + count, :size] = one[:, size:]
            at += count
        values[:, size:] = jnp.ones((total, size), BF16)

        @pl.when(pl.program_id(0) == 0)
        def _():
            me = flags_ref[0]
            row = lax.broadcasted_iota(jnp.int32, (length, length), 0)
            column = lax.broadcasted_iota(jnp.int32, (length, length), 1)
            ahead = column - row
            for k in range(total // length):
                source = me ^ (k ^ turn)
                late = ahead + (source - me) * length > 0
                bias[:, k * length : (k + 1) * length] = jnp.where(late, MASKED, 0.0)

        for h in range(heads):
            at = slice(h * size, (h + 1) * size)
            scores = lax.dot_general(
                query_ref[:, at], keys[...], (((1,), (1,)), ((), ())), preferred_element_type=F32
            )
            scores = scores * scale + bias[...]
            weights = jnp.exp2(scores - jnp.max(scores, axis=-1, keepdims=True))
            mixed = jnp.dot(weights.astype(BF16), values[...], preferred_element_type=F32)
            out_ref[:, at] = (mixed[:, :size] / mixed[:, size:]).astype(BF16)

    place = lambda g, f: (0, g if which is None else (f[1] ^ which) * groups + g)
    block = pl.BlockSpec((length, heads * size), place)
    return pl.pallas_call(
        kernel,
        grid_spec=pltpu.PrefetchScalarGridSpec(
            num_scalar_prefetch=1,
            grid=(groups,),
            in_specs=[block]
            + [pl.BlockSpec((one.shape[0], 2 * size), lambda g, f: (0, g)) for one in pieces]
            + [any_spec] * len(given),
            out_specs=block,
            scratch_shapes=[
                pltpu.VMEM((total, size), BF16),
                pltpu.VMEM((total, 2 * size), BF16),
                pltpu.VMEM((length, total), F32),
            ],
        ),
        out_shape=shape(soft_query.shape, BF16),
        input_output_aliases={2 + len(pieces): 0} if given else {},
        compiler_params=params(12),
        cost_estimate=cost(
            4 * groups * heads * size * length * total, 4 * length * groups * heads * size
        ),
    )(flags, soft_query, *pieces, *given)


def on_device(
    lin_query, lin_key, lin_value, log_decay, lin_gain,
    moe_input, routes, route_weight, gate_weight, up_weight, down_weight,
    soft_query, soft_kv,
):
    count, planes = lax.axis_size("ctx"), lax.axis_size("exp")
    me = lax.axis_index("ctx").astype(jnp.int32)
    flags = jnp.stack([me, me & 1, lax.axis_index("exp").astype(jnp.int32)])
    high = list(range(1, count.bit_length() - 1))
    chips = range(2, count, 2)
    experts = gate_weight.shape[0] * planes
    groups, size = soft_kv.shape[1], soft_kv.shape[3]
    heads = soft_query.shape[1] // size // groups
    split = groups % 2 == 0
    kv_width = groups * 2 * size
    after = lambda value: tie(flags, value)[0]

    held = soft_kv.reshape(soft_kv.shape[0], kv_width)
    kv_other = held
    if split:
        odd = flags[1] == 1
        first, second = held[:, : kv_width // 2], held[:, kv_width // 2 :]
        held, kv_other = jnp.where(odd, second, first), jnp.where(odd, first, second)

    outgoing = pack(tie(flags, held)[0], moe_input, routes, planes, experts)
    arrived = [outgoing[0]] + [swap(outgoing[p], "exp", p) for p in range(1, planes)]
    kv_other = tie(kv_other, outgoing[0])[0]
    held = jnp.concatenate([held, swap(kv_other, "ctx", 1)])
    kv_got = [swap(held, "ctx", j) for j in chips]
    *arrived, held = tie(*arrived, held)

    own, other = arrange(arrived)
    rows = jnp.concatenate([own, swap(other, "ctx", 1)])
    got = [swap(rows, "ctx", j) for j in chips]
    mine, factor, message, own_gate, other_gate = local_states(
        after(rows), lin_key, lin_value, log_decay, gate_weight
    )
    *got, message = tie(*got, message)
    near = jnp.concatenate([rows, *got])
    far = swap(near, "ctx", 1)
    neighbour = swap(message, "ctx", 1)

    sums = gate_and_up(flags, 0, near, own_gate, up_weight)
    total, total_factor, message = join_pair(after(sums[0]), mine, factor, neighbour)
    far, message = tie(far, message)
    before = before_factor = got = None
    if high:
        got = swap(message, "ctx", 2)
    inner, early = gate_and_up(
        flags, 1, far, other_gate, up_weight, sums, down_weight
    )
    for i, b in enumerate(high[:-1]):
        total, total_factor, message, before, before_factor = join_group(
            after(inner), b, total, total_factor, before, before_factor, got
        )
        got = swap(message, "ctx", 1 << high[i + 1])
    inner, message = tie(inner, message)
    send, early = down(flags, 1, inner, early, down_weight)
    summed = swap(send, "ctx", 1)
    keep, = down(after(send), 0, inner, early, down_weight)

    keep, *sends = fold_pair(keep, summed, count // 2)
    got_sums = [swap(one, "ctx", j) for j, one in zip(chips, sends)]
    attention = functools.partial(softmax_layer, size=size, heads=heads)
    pieces = [held, *kv_got]
    if split:
        whole = jnp.concatenate(tie(keep, *pieces)[1:])
        kv_far = swap(whole, "ctx", 1)
        soft_out = attention(after(sends[0]), 0, soft_query, [whole], 0, groups // 2)
        soft_out = attention(
            after(soft_out), 1, soft_query, [kv_far], 1, groups // 2, so_far=soft_out
        )
    else:
        soft_out = attention(after(sends[0]), None, soft_query, pieces, 0, groups)
    *got_sums, soft_out = tie(*got_sums, soft_out)
    own, send = fold_all(keep, got_sums)
    other = swap(send, "ctx", 1)
    last = high[-1] if high else 0
    state_near, state_send = join_end(
        after(send), last, before, before_factor, got, mine, factor, neighbour
    )
    state_far = swap(state_send, "ctx", 1)
    result = finish(own, other, planes)
    returned = [result[0]] + [swap(result[p], "exp", p) for p in range(1, planes)]
    lin_out = lightning(
        after(result[0]), lin_query, lin_key, lin_value, log_decay, lin_gain,
        state_near, state_far,
    )
    *returned, lin_out = tie(*returned, lin_out)
    moe_out = unpack(flags, returned, routes, route_weight)
    return (lin_out, moe_out, soft_out)


def solution(mesh):
    placed = (
        P("ctx", "exp"),
        P("ctx", "exp"),
        P("ctx", "exp"),
        P("ctx", "exp"),
        P("exp"),
        P(("ctx", "exp"), None),
        P(("ctx", "exp"), None),
        P(("ctx", "exp"), None),
        P("exp", None, "ctx"),
        P("exp", None, "ctx"),
        P("exp", "ctx", None),
        P("ctx", "exp"),
        P("ctx", "exp", None, None),
    )

    return jax.shard_map(
        on_device,
        mesh=mesh,
        in_specs=placed,
        out_specs=(P("ctx", "exp"), P(("ctx", "exp"), None), P("ctx", "exp")),
        check_vma=False,
    )
```

```python
import functools
import math

import jax
import jax.numpy as jnp
from jax import lax
from jax.experimental import pallas as pl
from jax.experimental.pallas import tpu as pltpu
from jax.sharding import PartitionSpec as P


TOP = 2
CAP = 2
F32 = jnp.float32
BF16 = jnp.bfloat16
MASKED = -1e30


vmem_spec = pl.BlockSpec(memory_space=pltpu.VMEM)
smem_spec = pl.BlockSpec(memory_space=pltpu.SMEM)
any_spec = pl.BlockSpec(memory_space=pl.ANY)
hbm_spec = pl.BlockSpec(memory_space=pltpu.HBM)


def shape(dims, dtype):
    return jax.ShapeDtypeStruct(tuple(dims), dtype)


def params(mib):
    return pltpu.CompilerParams(vmem_limit_bytes=mib << 20)


def cost(flops, nbytes):
    return pl.CostEstimate(flops=flops, bytes_accessed=nbytes, transcendentals=0)


def swap(value, axis, offset):
    return lax.ppermute(value, axis, [(i, i ^ offset) for i in range(lax.axis_size(axis))])


def tie(*values):
    return lax.optimization_barrier(values)


def in_hbm(*values):
    return [pltpu.with_memory_space_constraint(one, pltpu.HBM) for one in values]


def slot_matrix(flags_ref, routes_ref, rows, slots, here, weight_ref=None):
    named = [[routes_ref[k, r] for k in range(TOP)] for r in range(rows)]
    flat = [one for row in named for one in row]
    at_slot = lax.broadcasted_iota(jnp.int32, (slots, rows), 0)
    at_row = lax.broadcasted_iota(jnp.int32, (slots, rows), 1)
    matrix = jnp.zeros((slots, rows), F32)
    for i, mine in enumerate(flat):
        rank = jnp.int32(0)
        for other in flat[:i]:
            rank = rank + (other == mine).astype(jnp.int32)
        place = (lax.div(mine, here) ^ flags_ref[2]) * here + lax.rem(mine, here)
        slot = place * CAP + rank
        value = 1.0 if weight_ref is None else weight_ref[i % TOP, i // TOP]
        matrix = matrix + jnp.where((at_slot == slot) & (at_row == i // TOP), value, 0.0)
    return matrix


def pack(flags, moe_input, routes, planes, experts):
    rows, width = moe_input.shape
    slots = experts * CAP
    part = width // 2
    each = slots // planes

    def kernel(flags_ref, routes_ref, x_ref, *out_refs):
        matrix = slot_matrix(flags_ref, routes_ref, rows, slots, experts // planes)
        matrix = matrix.astype(BF16)
        for h in range(2):
            at = pl.ds(pl.multiple_of((flags_ref[1] ^ h) * part, 128), part)
            value = jnp.dot(matrix, x_ref[:, at], preferred_element_type=F32)
            for p, out_ref in enumerate(out_refs):
                out_ref[:, h * part : (h + 1) * part] = value[p * each : (p + 1) * each].astype(BF16)

    return pl.pallas_call(
        kernel,
        in_specs=[smem_spec, smem_spec, vmem_spec],
        out_specs=[vmem_spec] * planes,
        out_shape=[shape((each, width), BF16)] * planes,
        compiler_params=params(2),
    )(flags, *in_hbm(routes.T, moe_input))


def arrange(arrived):
    each, width = arrived[0].shape
    part = width // 2

    def kernel(*refs):
        *in_refs, own_ref, other_ref = refs
        for h, out_ref in enumerate((own_ref, other_ref)):
            at = slice(h * part, (h + 1) * part)
            out_ref[...] = jnp.concatenate([one[:, at].astype(F32) for one in in_refs]).astype(BF16)

    return pl.pallas_call(
        kernel,
        in_specs=[vmem_spec] * len(arrived),
        out_specs=[vmem_spec] * 2,
        out_shape=[shape((len(arrived) * each, part), BF16)] * 2,
        compiler_params=params(2),
    )(*arrived)


def unpack(flags, returned, routes, route_weight):
    planes = len(returned)
    each, width = returned[0].shape
    slots = planes * each
    rows = routes.shape[0]
    part = width // 2

    def kernel(flags_ref, routes_ref, weight_ref, *refs):
        *y_refs, out_ref = refs
        matrix = slot_matrix(flags_ref, routes_ref, rows, slots, each // CAP, weight_ref)
        pieces = []
        for _ in range(3):
            pieces.append(matrix.astype(BF16))
            matrix = matrix - pieces[-1].astype(F32)
        for h in range(2):
            y = jnp.concatenate(
                [one[:, h * part : (h + 1) * part].astype(F32) for one in y_refs]
            ).astype(BF16)
            total = None
            for piece in pieces:
                term = lax.dot_general(
                    piece, y, (((0,), (0,)), ((), ())), preferred_element_type=F32
                )
                total = term if total is None else total + term
            at = pl.ds(pl.multiple_of((flags_ref[1] ^ h) * part, 128), part)
            out_ref[:, at] = total.astype(BF16)

    return pl.pallas_call(
        kernel,
        in_specs=[smem_spec] * 3 + [vmem_spec] * planes,
        out_specs=vmem_spec,
        out_shape=shape((rows, width), BF16),
        compiler_params=params(4),
    )(flags, routes.T, route_weight.T, *returned)


def divisor(total, most, unit=128):
    return max(d for d in range(unit, most + 1, unit) if total % d == 0)


PIECES = 2


def copies(source, target, sems):
    rows = target.shape[0]
    pieces = max(p for p in range(1, PIECES + 1) if rows % (8 * p) == 0)
    each = rows // pieces
    return [
        pltpu.make_async_copy(
            source.at[c * each : (c + 1) * each], target.at[c * each : (c + 1) * each], sems.at[c]
        )
        for c in range(pieces)
    ]


def gate_and_up(flags, which, x_half, gates, up_weight, sums=None, down_weight=None):
    rows, part = x_half.shape
    experts, _, hidden = up_weight.shape
    deep = divisor(part, 1536)
    chunks = part // deep
    final = sums is not None
    given = 1 if final else 0
    left = max(1, experts - given)
    ahead = columns_ahead(part)
    blocks = lax.axis_size("ctx")
    block = rows // blocks

    def kernel(flags_ref, x_ref, *refs):
        gate_refs, up_ref, refs = refs[: len(gates)], refs[len(gates)], refs[len(gates) + 1 :]
        if final:
            (gate_in, up_in, up_first, down_ref, inner_ref, early_ref,
             ups, sems, early_sems, x_held) = refs
        else:
            gate_out, up_out, next_ref, ups, sems, next_sem = refs
        half = flags_ref[1] ^ which

        def fetch(e, s):
            at = pl.ds(pl.multiple_of(half * part + s * deep, deep), deep)
            return pltpu.make_async_copy(up_ref.at[e, at], ups.at[e - given, s], sems.at[e - given, s])

        for e in range(given, experts):
            for s in range(chunks):
                fetch(e, s).start()
        if not final:
            rest = pl.ds(pl.multiple_of((1 - half) * part, part), part)
            following = copies(up_ref.at[0, rest], next_ref, next_sem)
            for copy in following:
                copy.start()
        if final:
            early = fetch_ahead(flags_ref[1] ^ 1, part, ahead, down_ref, early_ref, early_sems)
            for copy in early:
                copy.start()
            expert_of = lax.rem(
                lax.div(lax.broadcasted_iota(jnp.int32, (rows, 1), 0), CAP), experts
            )

        @pl.when(flags_ref[0] >= 0)
        def _():
            x_used = x_ref
            if final:
                for k in range(blocks):
                    x_held[k * block : (k + 1) * block] = x_ref[(k ^ 1) * block : ((k ^ 1) + 1) * block]
                x_used = x_held
            for e in range(experts):
                if len(gate_refs[0].shape) == 3:
                    weight = gate_refs[0][e]
                else:
                    weight = gate_refs[0][...] if e == 0 else gate_refs[1][e - 1]
                gate = jnp.dot(x_used[...], weight, preferred_element_type=F32)
                if final:
                    gated = gate_in[e] + gate
                else:
                    gate_out[e] = gate
                if e < given:
                    weight = up_first[...]
                else:
                    for s in range(chunks):
                        fetch(e, s).wait()
                    weight = ups[e - given].reshape(part, hidden)
                up = jnp.dot(x_used[...], weight, preferred_element_type=F32)
                if final:
                    value = gated / (1.0 + jnp.exp(-gated)) * (up_in[e] + up)
                    here = jnp.broadcast_to(expert_of, (rows, hidden)) == e
                    inner_ref[e] = jnp.where(here, value, 0.0).astype(BF16)
                else:
                    up_out[e] = up
            if final:
                for copy in early:
                    copy.wait()
            else:
                for copy in following:
                    copy.wait()

    partial = shape((experts, rows, hidden), F32)
    scratch = [
        pltpu.VMEM((left, chunks, deep, hidden), BF16),
        pltpu.SemaphoreType.DMA((left, chunks)),
    ]
    if final:
        out_shape = [
            pltpu.VMEM((experts, rows, hidden), BF16),
            pltpu.VMEM((experts, hidden, ahead), BF16),
        ]
        scratch = scratch + [
            pltpu.SemaphoreType.DMA((experts, PIECES)), pltpu.VMEM((rows, part), BF16)
        ]
        operands, specs = (*sums, *in_hbm(down_weight)), [vmem_spec] * 3 + [hbm_spec]
    else:
        out_shape = [partial, partial, pltpu.VMEM((part, hidden), BF16)]
        scratch = scratch + [pltpu.SemaphoreType.DMA((PIECES,))]
        operands, specs = (), []
    return pl.pallas_call(
        kernel,
        in_specs=[smem_spec, vmem_spec] + [vmem_spec] * len(gates) + [hbm_spec] + specs,
        out_specs=[vmem_spec] * len(out_shape),
        out_shape=out_shape,
        scratch_shapes=scratch,
        compiler_params=params(15),
        cost_estimate=cost(4 * rows * experts * part * hidden, 4 * experts * part * hidden),
    )(flags, x_half, *gates, *in_hbm(up_weight), *operands)


def down_step(part):
    return divisor(part, 1024)


def columns_ahead(part):
    wide = down_step(part)
    return max(1, (part // wide) * 2 // 3) * wide


def fetch_ahead(half, part, ahead, weight_ref, to_ref, sems):
    at = pl.ds(pl.multiple_of(half * part, 128), ahead)
    return [
        copy
        for e in range(to_ref.shape[0])
        for copy in copies(weight_ref.at[e, :, at], to_ref.at[e], sems.at[e])
    ]


def down(flags, which, inner, early, down_weight):
    experts, rows, hidden = inner.shape
    part = down_weight.shape[2] // 2
    wide = down_step(part)
    ahead = early.shape[2]
    done = ahead // wide
    steps = part // wide
    left = max(1, steps - done)
    block = rows // lax.axis_size("ctx")

    def kernel(flags_ref, inner_ref, early_ref, down_ref, out_ref, *refs):
        if which == 1:
            next_ref, downs, sems, next_sems = refs
        else:
            downs, sems = refs
        half = flags_ref[1] ^ which

        def fetch(i):
            at = pl.ds(pl.multiple_of(half * part + i * wide, 128), wide)
            return [
                copy
                for e in range(experts)
                for copy in copies(
                    down_ref.at[e, :, at], downs.at[i - done, e], sems.at[i - done, e]
                )
            ]

        for i in range(done, steps):
            for copy in fetch(i):
                copy.start()
        if which == 1:
            following = fetch_ahead(flags_ref[1], part, ahead, down_ref, next_ref, next_sems)
            for copy in following:
                copy.start()

        @pl.when(flags_ref[0] >= 0)
        def _():
            for i in range(steps):
                if i >= done:
                    for copy in fetch(i):
                        copy.wait()
                total = None
                for e in range(experts):
                    weight = early_ref[e, :, i * wide : (i + 1) * wide] if i < done else downs[i - done, e]
                    term = jnp.dot(inner_ref[e], weight, preferred_element_type=F32)
                    total = term if total is None else total + term
                at = slice(i * wide, (i + 1) * wide)
                if which == 0:
                    out_ref[:, at] = total
                else:
                    for k in range(rows // block):
                        out_ref[k * block : (k + 1) * block, at] = total[
                            (k ^ 1) * block : ((k ^ 1) + 1) * block
                        ].astype(BF16)
            if which == 1:
                for copy in following:
                    copy.wait()

    scratch = [
        pltpu.VMEM((left, experts, hidden, wide), BF16),
        pltpu.SemaphoreType.DMA((left, experts, PIECES)),
    ]
    out_shape = [shape((rows, part), BF16 if which == 1 else F32)]
    if which == 1:
        out_shape.append(pltpu.VMEM((experts, hidden, ahead), BF16))
        scratch.append(pltpu.SemaphoreType.DMA((experts, PIECES)))
    return pl.pallas_call(
        kernel,
        in_specs=[smem_spec, vmem_spec, vmem_spec, hbm_spec],
        out_specs=[vmem_spec] * len(out_shape),
        out_shape=out_shape,
        scratch_shapes=scratch,
        compiler_params=params(12),
        cost_estimate=cost(rows * experts * 2 * part * hidden, 2 * experts * part * hidden),
    )(flags, inner, early, *in_hbm(down_weight))


def fold_pair(keep, got, pieces):
    rows, part = keep.shape
    each = rows // pieces

    def kernel(keep_ref, got_ref, out_ref, *send_refs):
        out_ref[...] = keep_ref[:each] + got_ref[:each].astype(F32)
        for k, send_ref in enumerate(send_refs, 1):
            at = slice(k * each, (k + 1) * each)
            send_ref[...] = (keep_ref[at] + got_ref[at].astype(F32)).astype(BF16)

    return pl.pallas_call(
        kernel,
        in_specs=[vmem_spec] * 2,
        out_specs=[vmem_spec] * pieces,
        out_shape=[shape((each, part), F32)] + [shape((each, part), BF16)] * (pieces - 1),
        compiler_params=params(4),
    )(keep, got)


def fold_all(keep, got):
    rows, part = keep.shape
    half = rows // 2

    def kernel(keep_ref, *refs):
        *got_refs, out_ref, send_ref = refs
        total = keep_ref[...]
        for one in got_refs:
            total = total + one[...].astype(F32)
        out_ref[...] = total[:half].astype(BF16)
        send_ref[...] = total[half:].astype(BF16)

    return pl.pallas_call(
        kernel,
        in_specs=[vmem_spec] * (1 + len(got)),
        out_specs=[vmem_spec] * 2,
        out_shape=[shape((half, part), BF16)] * 2,
        compiler_params=params(4),
    )(keep, *got)


def finish(own, other, planes):
    rows, part = own.shape
    each = rows // planes

    def kernel(own_ref, other_ref, *out_refs):
        for h, ref in enumerate((own_ref, other_ref)):
            value = ref[...].astype(F32)
            for p, out_ref in enumerate(out_refs):
                out_ref[:, h * part : (h + 1) * part] = value[p * each : (p + 1) * each].astype(BF16)

    return pl.pallas_call(
        kernel,
        in_specs=[vmem_spec] * 2,
        out_specs=[vmem_spec] * planes,
        out_shape=[shape((each, 2 * part), BF16)] * planes,
        compiler_params=params(2),
    )(own, other)


EXTRA = 8


def sums_of(decay_ref):
    length = decay_ref.shape[1]
    row = lax.broadcasted_iota(jnp.int32, (length, length), 0)
    column = lax.broadcasted_iota(jnp.int32, (length, length), 1)
    upper = (row <= column).astype(F32)
    across = jnp.dot(
        decay_ref[...], upper, precision=lax.Precision.HIGHEST, preferred_element_type=F32
    )
    return across.T, across


def put_message(ref, j, state, factor):
    size = state.shape[0]
    ref[j, :size] = state.astype(BF16)
    coarse = factor.astype(BF16)
    fine = (factor - coarse.astype(F32)).astype(BF16)
    which = lax.broadcasted_iota(jnp.int32, (EXTRA, state.shape[1]), 0)
    ref[j, size:] = jnp.where(
        which == 0, coarse.astype(F32), jnp.where(which == 1, fine.astype(F32), 0.0)
    ).astype(BF16)


def get_message(ref, j):
    size = ref.shape[1] - EXTRA
    state = ref[j, :size].astype(F32)
    tail = ref[j, size:].astype(F32)
    return state, tail[0:1] + tail[1:2]


def fetch_gate(flags, gate_weight):
    _, width, hidden = gate_weight.shape
    part = width // 2

    def kernel(flags_ref, gate_ref, out_ref, sems):
        at = pl.ds(pl.multiple_of(flags_ref[1] * part, part), part)
        under_way = copies(gate_ref.at[0, at], out_ref, sems)
        for copy in under_way:
            copy.start()
        for copy in under_way:
            copy.wait()

    return pl.pallas_call(
        kernel,
        in_specs=[smem_spec, hbm_spec],
        out_specs=vmem_spec,
        out_shape=pltpu.VMEM((part, hidden), BF16),
        scratch_shapes=[pltpu.SemaphoreType.DMA((PIECES,))],
        compiler_params=params(2),
        cost_estimate=cost(0, 2 * part * hidden),
    )(flags, *in_hbm(gate_weight))


def local_states(flags, lin_key, lin_value, log_decay, gate_weight):
    length, heads = log_decay.shape
    size = lin_key.shape[1] // heads
    half = heads // 2
    experts, width, hidden = gate_weight.shape
    part = width // 2
    counts = [experts] + ([experts - 1] if experts > 1 else [])

    def kernel(flags_ref, key_ref, value_ref, decay_ref, gate_ref, mine_ref, factor_ref, send_ref,
               *refs):
        *gate_outs, sems = refs
        step = pl.program_id(0)

        def fetch():
            for h, to in zip((1, 0), gate_outs):
                at = pl.ds(pl.multiple_of((flags_ref[1] ^ h) * part, part), part)
                for e in range(1 - h, experts):
                    yield from copies(gate_ref.at[e, at], to.at[e - (1 - h)], sems.at[h, e])

        @pl.when(step == 0)
        def _():
            for copy in fetch():
                copy.start()

        down, _ = sums_of(decay_ref)
        second = (flags_ref[1] ^ step) == 1
        down = jnp.where(second, down[:, half:], down[:, :half])
        last = down[length - 1 : length]
        tail = jnp.exp(last - down)
        factor = jnp.exp(last)
        for j in range(half):
            at = slice(j * size, (j + 1) * size)
            keyed = (key_ref[:, at].astype(F32) * tail[:, j : j + 1]).astype(BF16)
            state = lax.dot_general(
                keyed, value_ref[:, at], (((0,), (0,)), ((), ())), preferred_element_type=F32
            )
            whole = jnp.broadcast_to(factor[:, j : j + 1], (1, size))

            @pl.when(step == 0)
            def _():
                mine_ref[j] = state
                factor_ref[j : j + 1] = whole

            @pl.when(step == 1)
            def _():
                put_message(send_ref, j, state, whole)

        @pl.when(step == 1)
        def _():
            for copy in fetch():
                copy.wait()

    block = pl.BlockSpec((length, half * size), lambda i, p: (0, p[1] ^ i))
    full = lambda dims: pl.BlockSpec(dims, lambda i, p: (0,) * len(dims))
    return pl.pallas_call(
        kernel,
        grid_spec=pltpu.PrefetchScalarGridSpec(
            num_scalar_prefetch=1,
            grid=(2,),
            in_specs=[block, block, full((heads, length)), hbm_spec],
            out_specs=[
                full((half, size, size)),
                full((half, size)),
                full((half, size + EXTRA, size)),
            ]
            + [vmem_spec] * len(counts),
            scratch_shapes=[pltpu.SemaphoreType.DMA((2, experts, PIECES))],
        ),
        out_shape=[
            shape((half, size, size), F32),
            shape((half, size), F32),
            shape((half, size + EXTRA, size), BF16),
        ]
        + [pltpu.VMEM((one, part, hidden), BF16) for one in counts],
        compiler_params=params(3),
        cost_estimate=cost(
            4 * heads * length * size * size,
            4 * length * heads * size + 2 * experts * width * hidden,
        ),
    )(flags, *in_hbm(lin_key, lin_value, log_decay.T, gate_weight))


def join_pair(flags, mine, factor, got):
    half, size, _ = mine.shape

    def kernel(flags_ref, mine_ref, factor_ref, got_ref, sum_ref, sum_factor_ref, send_ref):
        odd = flags_ref[1] == 1
        for j in range(half):
            own, own_factor = mine_ref[j], factor_ref[j : j + 1]
            other, other_factor = get_message(got_ref, j)
            total = jnp.where(odd, own + own_factor * other, other + other_factor * own)
            both = own_factor * other_factor
            sum_ref[j] = total
            sum_factor_ref[j : j + 1] = both
            put_message(send_ref, j, total, both)

    return pl.pallas_call(
        kernel,
        in_specs=[smem_spec] + [vmem_spec] * 3,
        out_specs=[vmem_spec] * 3,
        out_shape=[
            shape((half, size, size), F32),
            shape((half, size), F32),
            shape((half, size + EXTRA, size), BF16),
        ],
        compiler_params=params(8),
    )(flags, mine, factor, got)


def join_group(flags, bit, total, factor, before, before_factor, got):
    half, size, _ = total.shape
    first = before is None
    earlier = () if first else (before, before_factor)

    def kernel(flags_ref, total_ref, factor_ref, got_ref, *refs):
        if first:
            sum_ref, sum_factor_ref, send_ref, before_out, before_factor_out = refs
        else:
            (before_ref, before_factor_ref,
             sum_ref, sum_factor_ref, send_ref, before_out, before_factor_out) = refs
        high = ((flags_ref[0] >> bit) & 1) == 1
        for j in range(half):
            own, own_factor = total_ref[j], factor_ref[j : j + 1]
            other, other_factor = get_message(got_ref, j)
            if first:
                prior, prior_factor = jnp.zeros_like(own), jnp.ones_like(own_factor)
            else:
                prior, prior_factor = before_ref[j], before_factor_ref[j : j + 1]
            before_out[j] = jnp.where(high, prior + prior_factor * other, prior)
            before_factor_out[j : j + 1] = jnp.where(
                high, prior_factor * other_factor, prior_factor
            )
            joined = jnp.where(high, own + own_factor * other, other + other_factor * own)
            both = own_factor * other_factor
            sum_ref[j] = joined
            sum_factor_ref[j : j + 1] = both
            put_message(send_ref, j, joined, both)

    return pl.pallas_call(
        kernel,
        in_specs=[smem_spec] + [vmem_spec] * (3 + len(earlier)),
        out_specs=[vmem_spec] * 5,
        out_shape=[
            shape((half, size, size), F32),
            shape((half, size), F32),
            shape((half, size + EXTRA, size), BF16),
            shape((half, size, size), F32),
            shape((half, size), F32),
        ],
        compiler_params=params(12),
    )(flags, total, factor, got, *earlier)


def join_end(flags, bit, before, before_factor, got, mine, factor, neighbour):
    half, size, _ = mine.shape
    given = [one for one in (before, before_factor, got) if one is not None]

    def kernel(flags_ref, *refs):
        refs = list(refs)
        before_ref = refs.pop(0) if before is not None else None
        before_factor_ref = refs.pop(0) if before is not None else None
        got_ref = refs.pop(0) if got is not None else None
        mine_ref, factor_ref, neighbour_ref, keep_ref, send_ref = refs
        high, odd = ((flags_ref[0] >> bit) & 1) == 1, flags_ref[1] == 1
        for j in range(half):
            state = jnp.zeros((size, size), F32)
            if before_ref is not None:
                state = before_ref[j]
            if got_ref is not None:
                other, _ = get_message(got_ref, j)
                scaled = other if before_ref is None else before_factor_ref[j : j + 1] * other
                state = jnp.where(high, state + scaled, state)
            other, other_factor = get_message(neighbour_ref, j)
            even_state = jnp.where(odd, other, mine_ref[j])
            even_factor = jnp.where(odd, other_factor, factor_ref[j : j + 1])
            for_odd = even_state + even_factor * state
            keep_ref[j] = jnp.where(odd, for_odd, state).astype(BF16)
            send_ref[j] = jnp.where(odd, state, for_odd).astype(BF16)

    return pl.pallas_call(
        kernel,
        in_specs=[smem_spec] + [vmem_spec] * (len(given) + 3),
        out_specs=[vmem_spec] * 2,
        out_shape=[shape((half, size, size), BF16)] * 2,
        compiler_params=params(8),
    )(flags, *given, mine, factor, neighbour)


def lightning(flags, lin_query, lin_key, lin_value, log_decay, lin_gain, near, far):
    length, heads = log_decay.shape
    size = lin_key.shape[1] // heads
    half = heads // 2
    scale = 1.0 / math.sqrt(size)

    def kernel(flags_ref, query_ref, key_ref, value_ref, decay_ref, gain_ref, near_ref, far_ref,
               out_ref):
        down, across = sums_of(decay_ref)
        step = pl.program_id(0)
        second = (flags_ref[1] ^ step) == 1
        down = jnp.where(second, down[:, half:], down[:, :half])
        across = jnp.where(second, across[half:], across[:half])
        risen = jnp.exp(down) * scale
        row = lax.broadcasted_iota(jnp.int32, (length, length), 0)
        column = lax.broadcasted_iota(jnp.int32, (length, length), 1)
        causal = column <= row
        for j in range(half):
            at = slice(j * size, (j + 1) * size)
            query, key, value = query_ref[:, at], key_ref[:, at], value_ref[:, at]
            scores = lax.dot_general(
                query, key, (((1,), (1,)), ((), ())), preferred_element_type=F32
            )
            spread = down[:, j : j + 1] - across[j : j + 1]
            decays = jnp.exp(jnp.where(causal, spread, MASKED))
            mixed = (scores * (decays * scale)).astype(BF16)
            prior = jnp.where(step == 0, near_ref[j], far_ref[j])
            combined = jnp.dot(mixed, value, preferred_element_type=F32)
            combined = combined + risen[:, j : j + 1] * jnp.dot(
                query, prior, preferred_element_type=F32
            )
            square = jnp.mean(combined * combined, axis=-1, keepdims=True) + 1e-06
            out_ref[:, at] = (combined * lax.rsqrt(square) * gain_ref[:, at]).astype(BF16)

    block = pl.BlockSpec((length, half * size), lambda i, p: (0, p[1] ^ i))
    gains = pl.BlockSpec((1, half * size), lambda i, p: (0, p[1] ^ i))
    full = lambda dims: pl.BlockSpec(dims, lambda i, p: (0,) * len(dims))
    return pl.pallas_call(
        kernel,
        grid_spec=pltpu.PrefetchScalarGridSpec(
            num_scalar_prefetch=1,
            grid=(2,),
            in_specs=[
                block, block, block, full((heads, length)), gains,
                full((half, size, size)), full((half, size, size)),
            ],
            out_specs=block,
        ),
        out_shape=shape(lin_query.shape, BF16),
        compiler_params=params(12),
        cost_estimate=cost(6 * heads * length * size * size, 8 * length * heads * size),
    )(flags, lin_query, lin_key, lin_value, log_decay.T, lin_gain.reshape(1, -1), near, far)


def softmax_layer(flags, which, soft_query, pieces, turn, groups, size, heads, so_far=None):
    length, _ = soft_query.shape
    total = sum(one.shape[0] for one in pieces)
    scale = math.log2(math.e) / math.sqrt(size)
    given = () if so_far is None else (so_far,)

    def kernel(flags_ref, query_ref, *refs):
        piece_refs = refs[: len(pieces)]
        out_ref, keys, values, bias = refs[len(pieces) + len(given) :]
        at = 0
        for one in piece_refs:
            count = one.shape[0]
            keys[at : at + count] = one[:, :size]
            values[at : at + count, :size] = one[:, size:]
            at += count
        values[:, size:] = jnp.ones((total, size), BF16)

        @pl.when(pl.program_id(0) == 0)
        def _():
            me = flags_ref[0]
            row = lax.broadcasted_iota(jnp.int32, (length, length), 0)
            column = lax.broadcasted_iota(jnp.int32, (length, length), 1)
            ahead = column - row
            for k in range(total // length):
                source = me ^ (k ^ turn)
                late = ahead + (source - me) * length > 0
                bias[:, k * length : (k + 1) * length] = jnp.where(late, MASKED, 0.0)

        for h in range(heads):
            at = slice(h * size, (h + 1) * size)
            scores = lax.dot_general(
                query_ref[:, at], keys[...], (((1,), (1,)), ((), ())), preferred_element_type=F32
            )
            scores = scores * scale + bias[...]
            weights = jnp.exp2(scores - jnp.max(scores, axis=-1, keepdims=True))
            mixed = jnp.dot(weights.astype(BF16), values[...], preferred_element_type=F32)
            out_ref[:, at] = (mixed[:, :size] / mixed[:, size:]).astype(BF16)

    place = lambda g, f: (0, g if which is None else (f[1] ^ which) * groups + g)
    block = pl.BlockSpec((length, heads * size), place)
    return pl.pallas_call(
        kernel,
        grid_spec=pltpu.PrefetchScalarGridSpec(
            num_scalar_prefetch=1,
            grid=(groups,),
            in_specs=[block]
            + [pl.BlockSpec((one.shape[0], 2 * size), lambda g, f: (0, g)) for one in pieces]
            + [any_spec] * len(given),
            out_specs=block,
            scratch_shapes=[
                pltpu.VMEM((total, size), BF16),
                pltpu.VMEM((total, 2 * size), BF16),
                pltpu.VMEM((length, total), F32),
            ],
        ),
        out_shape=shape(soft_query.shape, BF16),
        input_output_aliases={2 + len(pieces): 0} if given else {},
        compiler_params=params(12),
        cost_estimate=cost(
            4 * groups * heads * size * length * total, 4 * length * groups * heads * size
        ),
    )(flags, soft_query, *pieces, *given)


def on_device(
    lin_query, lin_key, lin_value, log_decay, lin_gain,
    moe_input, routes, route_weight, gate_weight, up_weight, down_weight,
    soft_query, soft_kv,
):
    count, planes = lax.axis_size("ctx"), lax.axis_size("exp")
    me = lax.axis_index("ctx").astype(jnp.int32)
    flags = jnp.stack([me, me & 1, lax.axis_index("exp").astype(jnp.int32)])
    high = list(range(1, count.bit_length() - 1))
    chips = range(2, count, 2)
    experts = gate_weight.shape[0] * planes
    groups, size = soft_kv.shape[1], soft_kv.shape[3]
    heads = soft_query.shape[1] // size // groups
    split = groups % 2 == 0
    kv_width = groups * 2 * size
    after = lambda value: tie(flags, value)[0]

    outgoing = pack(flags, moe_input, routes, planes, experts)
    soft_kv = tie(soft_kv, outgoing[0])[0]
    held = soft_kv.reshape(soft_kv.shape[0], kv_width)
    kv_other = held
    if split:
        odd = flags[1] == 1
        first, second = held[:, : kv_width // 2], held[:, kv_width // 2 :]
        held, kv_other = jnp.where(odd, second, first), jnp.where(odd, first, second)
    arrived = [outgoing[0]] + [swap(outgoing[p], "exp", p) for p in range(1, planes)]
    held = jnp.concatenate([held, swap(kv_other, "ctx", 1)])
    kv_got = [swap(held, "ctx", j) for j in chips]
    gate_first = fetch_gate(after(held), gate_weight)
    *arrived, held, gate_first = tie(*arrived, held, gate_first)

    own, other = arrange(arrived)
    rows = jnp.concatenate([own, swap(other, "ctx", 1)])
    got = [swap(rows, "ctx", j) for j in chips]
    mine, factor, message, other_gate, *own_rest = local_states(
        after(rows), lin_key, lin_value, log_decay, gate_weight
    )
    *got, message = tie(*got, message)
    near = jnp.concatenate([rows, *got])
    far = swap(near, "ctx", 1)
    neighbour = swap(message, "ctx", 1)

    sums = gate_and_up(flags, 0, near, [gate_first, *own_rest], up_weight)
    total, total_factor, message = join_pair(after(sums[0]), mine, factor, neighbour)
    far, message = tie(far, message)
    before = before_factor = got = None
    if high:
        got = swap(message, "ctx", 2)
    inner, early = gate_and_up(
        flags, 1, far, [other_gate], up_weight, sums, down_weight
    )
    for i, b in enumerate(high[:-1]):
        total, total_factor, message, before, before_factor = join_group(
            after(inner), b, total, total_factor, before, before_factor, got
        )
        got = swap(message, "ctx", 1 << high[i + 1])
    inner, message = tie(inner, message)
    send, early = down(flags, 1, inner, early, down_weight)
    summed = swap(send, "ctx", 1)
    keep, = down(after(send), 0, inner, early, down_weight)

    keep, *sends = fold_pair(keep, summed, count // 2)
    got_sums = [swap(one, "ctx", j) for j, one in zip(chips, sends)]
    attention = functools.partial(softmax_layer, size=size, heads=heads)
    pieces = [held, *kv_got]
    if split:
        whole = jnp.concatenate(tie(keep, *pieces)[1:])
        kv_far = swap(whole, "ctx", 1)
        soft_out = attention(after(sends[0]), 0, soft_query, [whole], 0, groups // 2)
        soft_out = attention(
            after(soft_out), 1, soft_query, [kv_far], 1, groups // 2, so_far=soft_out
        )
    else:
        soft_out = attention(after(sends[0]), None, soft_query, pieces, 0, groups)
    *got_sums, soft_out = tie(*got_sums, soft_out)
    own, send = fold_all(keep, got_sums)
    other = swap(send, "ctx", 1)
    last = high[-1] if high else 0
    state_near, state_send = join_end(
        after(send), last, before, before_factor, got, mine, factor, neighbour
    )
    state_far = swap(state_send, "ctx", 1)
    result = finish(own, other, planes)
    returned = [result[0]] + [swap(result[p], "exp", p) for p in range(1, planes)]
    lin_out = lightning(
        after(result[0]), lin_query, lin_key, lin_value, log_decay, lin_gain,
        state_near, state_far,
    )
    *returned, lin_out = tie(*returned, lin_out)
    moe_out = unpack(flags, returned, routes, route_weight)
    return (lin_out, moe_out, soft_out)


def solution(mesh):
    placed = (
        P("ctx", "exp"),
        P("ctx", "exp"),
        P("ctx", "exp"),
        P("ctx", "exp"),
        P("exp"),
        P(("ctx", "exp"), None),
        P(("ctx", "exp"), None),
        P(("ctx", "exp"), None),
        P("exp", None, "ctx"),
        P("exp", None, "ctx"),
        P("exp", "ctx", None),
        P("ctx", "exp"),
        P("ctx", "exp", None, None),
    )

    return jax.shard_map(
        on_device,
        mesh=mesh,
        in_specs=placed,
        out_specs=(P("ctx", "exp"), P(("ctx", "exp"), None), P("ctx", "exp")),
        check_vma=False,
    )
```

```python
import functools
import math

import jax
import jax.numpy as jnp
from jax import lax
from jax.experimental import pallas as pl
from jax.experimental.pallas import tpu as pltpu
from jax.sharding import PartitionSpec as P


TOP = 2
CAP = 2
F32 = jnp.float32
BF16 = jnp.bfloat16
MASKED = -1e30


vmem_spec = pl.BlockSpec(memory_space=pltpu.VMEM)
smem_spec = pl.BlockSpec(memory_space=pltpu.SMEM)
any_spec = pl.BlockSpec(memory_space=pl.ANY)
hbm_spec = pl.BlockSpec(memory_space=pltpu.HBM)


def shape(dims, dtype):
    return jax.ShapeDtypeStruct(tuple(dims), dtype)


def params(mib):
    return pltpu.CompilerParams(vmem_limit_bytes=mib << 20)


def cost(flops, nbytes):
    return pl.CostEstimate(flops=flops, bytes_accessed=nbytes, transcendentals=0)


def swap(value, axis, offset):
    return lax.ppermute(value, axis, [(i, i ^ offset) for i in range(lax.axis_size(axis))])


def tie(*values):
    return lax.optimization_barrier(values)


def in_hbm(*values):
    return [pltpu.with_memory_space_constraint(one, pltpu.HBM) for one in values]


def slot_matrix(flags_ref, routes_ref, rows, slots, here, weight_ref=None):
    named = [[routes_ref[k, r] for k in range(TOP)] for r in range(rows)]
    flat = [one for row in named for one in row]
    at_slot = lax.broadcasted_iota(jnp.int32, (slots, rows), 0)
    at_row = lax.broadcasted_iota(jnp.int32, (slots, rows), 1)
    matrix = jnp.zeros((slots, rows), F32)
    for i, mine in enumerate(flat):
        rank = jnp.int32(0)
        for other in flat[:i]:
            rank = rank + (other == mine).astype(jnp.int32)
        place = (lax.div(mine, here) ^ flags_ref[2]) * here + lax.rem(mine, here)
        slot = place * CAP + rank
        value = 1.0 if weight_ref is None else weight_ref[i % TOP, i // TOP]
        matrix = matrix + jnp.where((at_slot == slot) & (at_row == i // TOP), value, 0.0)
    return matrix


def pack(flags, moe_input, routes, planes, experts):
    rows, width = moe_input.shape
    slots = experts * CAP
    part = width // 2
    each = slots // planes

    def kernel(flags_ref, routes_ref, x_ref, *out_refs):
        matrix = slot_matrix(flags_ref, routes_ref, rows, slots, experts // planes)
        matrix = matrix.astype(BF16)
        for h in range(2):
            at = pl.ds(pl.multiple_of((flags_ref[1] ^ h) * part, 128), part)
            value = jnp.dot(matrix, x_ref[:, at], preferred_element_type=F32)
            for p, out_ref in enumerate(out_refs):
                out_ref[:, h * part : (h + 1) * part] = value[p * each : (p + 1) * each].astype(BF16)

    return pl.pallas_call(
        kernel,
        in_specs=[smem_spec, smem_spec, vmem_spec],
        out_specs=[vmem_spec] * planes,
        out_shape=[shape((each, width), BF16)] * planes,
        compiler_params=params(2),
    )(flags, *in_hbm(routes.T, moe_input))


def arrange(arrived):
    each, width = arrived[0].shape
    part = width // 2

    def kernel(*refs):
        *in_refs, own_ref, other_ref = refs
        for h, out_ref in enumerate((own_ref, other_ref)):
            at = slice(h * part, (h + 1) * part)
            out_ref[...] = jnp.concatenate([one[:, at].astype(F32) for one in in_refs]).astype(BF16)

    return pl.pallas_call(
        kernel,
        in_specs=[vmem_spec] * len(arrived),
        out_specs=[vmem_spec] * 2,
        out_shape=[shape((len(arrived) * each, part), BF16)] * 2,
        compiler_params=params(2),
    )(*arrived)


def unpack(flags, returned, routes, route_weight):
    planes = len(returned)
    each, width = returned[0].shape
    slots = planes * each
    rows = routes.shape[0]
    part = width // 2

    def kernel(flags_ref, routes_ref, weight_ref, *refs):
        *y_refs, out_ref = refs
        matrix = slot_matrix(flags_ref, routes_ref, rows, slots, each // CAP, weight_ref)
        pieces = []
        for _ in range(3):
            pieces.append(matrix.astype(BF16))
            matrix = matrix - pieces[-1].astype(F32)
        for h in range(2):
            y = jnp.concatenate(
                [one[:, h * part : (h + 1) * part].astype(F32) for one in y_refs]
            ).astype(BF16)
            total = None
            for piece in pieces:
                term = lax.dot_general(
                    piece, y, (((0,), (0,)), ((), ())), preferred_element_type=F32
                )
                total = term if total is None else total + term
            at = pl.ds(pl.multiple_of((flags_ref[1] ^ h) * part, 128), part)
            out_ref[:, at] = total.astype(BF16)

    return pl.pallas_call(
        kernel,
        in_specs=[smem_spec] * 3 + [vmem_spec] * planes,
        out_specs=vmem_spec,
        out_shape=shape((rows, width), BF16),
        compiler_params=params(4),
    )(flags, routes.T, route_weight.T, *returned)


def divisor(total, most, unit=128):
    return max(d for d in range(unit, most + 1, unit) if total % d == 0)


PIECES = 2


def copies(source, target, sems, most=PIECES):
    rows = target.shape[0]
    pieces = max(p for p in range(1, most + 1) if rows % (8 * p) == 0)
    each = rows // pieces
    return [
        pltpu.make_async_copy(
            source.at[c * each : (c + 1) * each], target.at[c * each : (c + 1) * each], sems.at[c]
        )
        for c in range(pieces)
    ]


def gate_and_up(flags, which, x_half, gates, up_weight, sums=None, down_weight=None):
    rows, part = x_half.shape
    experts, _, hidden = up_weight.shape
    deep = divisor(part, 1536)
    chunks = part // deep
    final = sums is not None
    given = 1 if final else 0
    left = max(1, experts - given)
    ahead = columns_ahead(part)
    blocks = lax.axis_size("ctx")
    block = rows // blocks

    def kernel(flags_ref, x_ref, *refs):
        gate_refs, up_ref, refs = refs[: len(gates)], refs[len(gates)], refs[len(gates) + 1 :]
        if final:
            (gate_in, up_in, up_first, down_ref, inner_ref, early_ref,
             ups, sems, early_sems, x_held) = refs
        else:
            gate_out, up_out, next_ref, ups, sems, next_sem = refs
        half = flags_ref[1] ^ which

        def fetch(e, s):
            at = pl.ds(pl.multiple_of(half * part + s * deep, deep), deep)
            return pltpu.make_async_copy(up_ref.at[e, at], ups.at[e - given, s], sems.at[e - given, s])

        for e in range(given, experts):
            for s in range(chunks):
                fetch(e, s).start()
        if not final:
            rest = pl.ds(pl.multiple_of((1 - half) * part, part), part)
            following = copies(up_ref.at[0, rest], next_ref, next_sem)
            for copy in following:
                copy.start()
        if final:
            early = fetch_ahead(flags_ref[1] ^ 1, part, ahead, down_ref, early_ref, early_sems)
            for copy in early:
                copy.start()
            expert_of = lax.rem(
                lax.div(lax.broadcasted_iota(jnp.int32, (rows, 1), 0), CAP), experts
            )

        @pl.when(flags_ref[0] >= 0)
        def _():
            x_used = x_ref
            if final:
                for k in range(blocks):
                    x_held[k * block : (k + 1) * block] = x_ref[(k ^ 1) * block : ((k ^ 1) + 1) * block]
                x_used = x_held
            for e in range(experts):
                if len(gate_refs[0].shape) == 3:
                    weight = gate_refs[0][e]
                else:
                    weight = gate_refs[0][...] if e == 0 else gate_refs[1][e - 1]
                gate = jnp.dot(x_used[...], weight, preferred_element_type=F32)
                if final:
                    gated = gate_in[e] + gate
                else:
                    gate_out[e] = gate
                if e < given:
                    weight = up_first[...]
                else:
                    for s in range(chunks):
                        fetch(e, s).wait()
                    weight = ups[e - given].reshape(part, hidden)
                up = jnp.dot(x_used[...], weight, preferred_element_type=F32)
                if final:
                    value = gated / (1.0 + jnp.exp(-gated)) * (up_in[e] + up)
                    here = jnp.broadcast_to(expert_of, (rows, hidden)) == e
                    inner_ref[e] = jnp.where(here, value, 0.0).astype(BF16)
                else:
                    up_out[e] = up
            if final:
                for copy in early:
                    copy.wait()
            else:
                for copy in following:
                    copy.wait()

    partial = shape((experts, rows, hidden), F32)
    scratch = [
        pltpu.VMEM((left, chunks, deep, hidden), BF16),
        pltpu.SemaphoreType.DMA((left, chunks)),
    ]
    if final:
        out_shape = [
            pltpu.VMEM((experts, rows, hidden), BF16),
            pltpu.VMEM((experts, hidden, ahead), BF16),
        ]
        scratch = scratch + [
            pltpu.SemaphoreType.DMA((experts, PIECES)), pltpu.VMEM((rows, part), BF16)
        ]
        operands, specs = (*sums, *in_hbm(down_weight)), [vmem_spec] * 3 + [hbm_spec]
    else:
        out_shape = [partial, partial, pltpu.VMEM((part, hidden), BF16)]
        scratch = scratch + [pltpu.SemaphoreType.DMA((PIECES,))]
        operands, specs = (), []
    return pl.pallas_call(
        kernel,
        in_specs=[smem_spec, vmem_spec] + [vmem_spec] * len(gates) + [hbm_spec] + specs,
        out_specs=[vmem_spec] * len(out_shape),
        out_shape=out_shape,
        scratch_shapes=scratch,
        compiler_params=params(15),
        cost_estimate=cost(4 * rows * experts * part * hidden, 4 * experts * part * hidden),
    )(flags, x_half, *gates, *in_hbm(up_weight), *operands)


def down_step(part):
    return divisor(part, 1024)


def columns_ahead(part):
    wide = down_step(part)
    return max(1, (part // wide) * 2 // 3) * wide


def fetch_ahead(half, part, ahead, weight_ref, to_ref, sems):
    at = pl.ds(pl.multiple_of(half * part, 128), ahead)
    return [
        copy
        for e in range(to_ref.shape[0])
        for copy in copies(weight_ref.at[e, :, at], to_ref.at[e], sems.at[e])
    ]


def down(flags, which, inner, early, down_weight):
    experts, rows, hidden = inner.shape
    part = down_weight.shape[2] // 2
    wide = down_step(part)
    ahead = early.shape[2]
    done = ahead // wide
    steps = part // wide
    left = max(1, steps - done)
    block = rows // lax.axis_size("ctx")

    def kernel(flags_ref, inner_ref, early_ref, down_ref, out_ref, *refs):
        if which == 1:
            next_ref, downs, sems, next_sems = refs
        else:
            downs, sems = refs
        half = flags_ref[1] ^ which

        def fetch(i):
            at = pl.ds(pl.multiple_of(half * part + i * wide, 128), wide)
            return [
                copy
                for e in range(experts)
                for copy in copies(
                    down_ref.at[e, :, at], downs.at[i - done, e], sems.at[i - done, e]
                )
            ]

        for i in range(done, steps):
            for copy in fetch(i):
                copy.start()
        if which == 1:
            following = fetch_ahead(flags_ref[1], part, ahead, down_ref, next_ref, next_sems)
            for copy in following:
                copy.start()

        @pl.when(flags_ref[0] >= 0)
        def _():
            for i in range(steps):
                if i >= done:
                    for copy in fetch(i):
                        copy.wait()
                total = None
                for e in range(experts):
                    weight = early_ref[e, :, i * wide : (i + 1) * wide] if i < done else downs[i - done, e]
                    term = jnp.dot(inner_ref[e], weight, preferred_element_type=F32)
                    total = term if total is None else total + term
                at = slice(i * wide, (i + 1) * wide)
                if which == 0:
                    out_ref[:, at] = total
                else:
                    for k in range(rows // block):
                        out_ref[k * block : (k + 1) * block, at] = total[
                            (k ^ 1) * block : ((k ^ 1) + 1) * block
                        ].astype(BF16)
            if which == 1:
                for copy in following:
                    copy.wait()

    scratch = [
        pltpu.VMEM((left, experts, hidden, wide), BF16),
        pltpu.SemaphoreType.DMA((left, experts, PIECES)),
    ]
    out_shape = [shape((rows, part), BF16 if which == 1 else F32)]
    if which == 1:
        out_shape.append(pltpu.VMEM((experts, hidden, ahead), BF16))
        scratch.append(pltpu.SemaphoreType.DMA((experts, PIECES)))
    return pl.pallas_call(
        kernel,
        in_specs=[smem_spec, vmem_spec, vmem_spec, hbm_spec],
        out_specs=[vmem_spec] * len(out_shape),
        out_shape=out_shape,
        scratch_shapes=scratch,
        compiler_params=params(12),
        cost_estimate=cost(rows * experts * 2 * part * hidden, 2 * experts * part * hidden),
    )(flags, inner, early, *in_hbm(down_weight))


def fold_pair(keep, got, pieces):
    rows, part = keep.shape
    each = rows // pieces

    def kernel(keep_ref, got_ref, out_ref, *send_refs):
        out_ref[...] = keep_ref[:each] + got_ref[:each].astype(F32)
        for k, send_ref in enumerate(send_refs, 1):
            at = slice(k * each, (k + 1) * each)
            send_ref[...] = (keep_ref[at] + got_ref[at].astype(F32)).astype(BF16)

    return pl.pallas_call(
        kernel,
        in_specs=[vmem_spec] * 2,
        out_specs=[vmem_spec] * pieces,
        out_shape=[shape((each, part), F32)] + [shape((each, part), BF16)] * (pieces - 1),
        compiler_params=params(4),
    )(keep, got)


def fold_all(keep, got):
    rows, part = keep.shape
    half = rows // 2

    def kernel(keep_ref, *refs):
        *got_refs, out_ref, send_ref = refs
        total = keep_ref[...]
        for one in got_refs:
            total = total + one[...].astype(F32)
        out_ref[...] = total[:half].astype(BF16)
        send_ref[...] = total[half:].astype(BF16)

    return pl.pallas_call(
        kernel,
        in_specs=[vmem_spec] * (1 + len(got)),
        out_specs=[vmem_spec] * 2,
        out_shape=[shape((half, part), BF16)] * 2,
        compiler_params=params(4),
    )(keep, *got)


def finish(own, other, planes):
    rows, part = own.shape
    each = rows // planes

    def kernel(own_ref, other_ref, *out_refs):
        for h, ref in enumerate((own_ref, other_ref)):
            value = ref[...].astype(F32)
            for p, out_ref in enumerate(out_refs):
                out_ref[:, h * part : (h + 1) * part] = value[p * each : (p + 1) * each].astype(BF16)

    return pl.pallas_call(
        kernel,
        in_specs=[vmem_spec] * 2,
        out_specs=[vmem_spec] * planes,
        out_shape=[shape((each, 2 * part), BF16)] * planes,
        compiler_params=params(2),
    )(own, other)


EXTRA = 8


def sums_of(decay_ref):
    length = decay_ref.shape[1]
    row = lax.broadcasted_iota(jnp.int32, (length, length), 0)
    column = lax.broadcasted_iota(jnp.int32, (length, length), 1)
    upper = (row <= column).astype(F32)
    across = jnp.dot(
        decay_ref[...], upper, precision=lax.Precision.HIGHEST, preferred_element_type=F32
    )
    return across.T, across


def put_message(ref, j, state, factor):
    size = state.shape[0]
    ref[j, :size] = state.astype(BF16)
    coarse = factor.astype(BF16)
    fine = (factor - coarse.astype(F32)).astype(BF16)
    which = lax.broadcasted_iota(jnp.int32, (EXTRA, state.shape[1]), 0)
    ref[j, size:] = jnp.where(
        which == 0, coarse.astype(F32), jnp.where(which == 1, fine.astype(F32), 0.0)
    ).astype(BF16)


def get_message(ref, j):
    size = ref.shape[1] - EXTRA
    state = ref[j, :size].astype(F32)
    tail = ref[j, size:].astype(F32)
    return state, tail[0:1] + tail[1:2]


def fetch_gate(flags, gate_weight):
    _, width, hidden = gate_weight.shape
    part = width // 2

    def kernel(flags_ref, gate_ref, out_ref, sems):
        at = pl.ds(pl.multiple_of(flags_ref[1] * part, part), part)
        under_way = copies(gate_ref.at[0, at], out_ref, sems, 6)
        for copy in under_way:
            copy.start()
        for copy in under_way:
            copy.wait()

    return pl.pallas_call(
        kernel,
        in_specs=[smem_spec, hbm_spec],
        out_specs=vmem_spec,
        out_shape=pltpu.VMEM((part, hidden), BF16),
        scratch_shapes=[pltpu.SemaphoreType.DMA((6,))],
        compiler_params=params(2),
        cost_estimate=cost(0, 2 * part * hidden),
    )(flags, *in_hbm(gate_weight))


def local_states(flags, lin_key, lin_value, log_decay, gate_weight):
    length, heads = log_decay.shape
    size = lin_key.shape[1] // heads
    half = heads // 2
    experts, width, hidden = gate_weight.shape
    part = width // 2
    counts = [experts] + ([experts - 1] if experts > 1 else [])

    def kernel(flags_ref, key_ref, value_ref, decay_ref, gate_ref, mine_ref, factor_ref, send_ref,
               *refs):
        *gate_outs, sems = refs
        step = pl.program_id(0)

        def fetch():
            for h, to in zip((1, 0), gate_outs):
                at = pl.ds(pl.multiple_of((flags_ref[1] ^ h) * part, part), part)
                for e in range(1 - h, experts):
                    yield from copies(gate_ref.at[e, at], to.at[e - (1 - h)], sems.at[h, e])

        @pl.when(step == 0)
        def _():
            for copy in fetch():
                copy.start()

        down, _ = sums_of(decay_ref)
        second = (flags_ref[1] ^ step) == 1
        down = jnp.where(second, down[:, half:], down[:, :half])
        last = down[length - 1 : length]
        tail = jnp.exp(last - down)
        factor = jnp.exp(last)
        for j in range(half):
            at = slice(j * size, (j + 1) * size)
            keyed = (key_ref[:, at].astype(F32) * tail[:, j : j + 1]).astype(BF16)
            state = lax.dot_general(
                keyed, value_ref[:, at], (((0,), (0,)), ((), ())), preferred_element_type=F32
            )
            whole = jnp.broadcast_to(factor[:, j : j + 1], (1, size))

            @pl.when(step == 0)
            def _():
                mine_ref[j] = state
                factor_ref[j : j + 1] = whole

            @pl.when(step == 1)
            def _():
                put_message(send_ref, j, state, whole)

        @pl.when(step == 1)
        def _():
            for copy in fetch():
                copy.wait()

    block = pl.BlockSpec((length, half * size), lambda i, p: (0, p[1] ^ i))
    full = lambda dims: pl.BlockSpec(dims, lambda i, p: (0,) * len(dims))
    return pl.pallas_call(
        kernel,
        grid_spec=pltpu.PrefetchScalarGridSpec(
            num_scalar_prefetch=1,
            grid=(2,),
            in_specs=[block, block, full((heads, length)), hbm_spec],
            out_specs=[
                full((half, size, size)),
                full((half, size)),
                full((half, size + EXTRA, size)),
            ]
            + [vmem_spec] * len(counts),
            scratch_shapes=[pltpu.SemaphoreType.DMA((2, experts, PIECES))],
        ),
        out_shape=[
            shape((half, size, size), F32),
            shape((half, size), F32),
            shape((half, size + EXTRA, size), BF16),
        ]
        + [pltpu.VMEM((one, part, hidden), BF16) for one in counts],
        compiler_params=params(3),
        cost_estimate=cost(
            4 * heads * length * size * size,
            4 * length * heads * size + 2 * experts * width * hidden,
        ),
    )(flags, *in_hbm(lin_key, lin_value, log_decay.T, gate_weight))


def join_pair(flags, mine, factor, got):
    half, size, _ = mine.shape

    def kernel(flags_ref, mine_ref, factor_ref, got_ref, send_ref):
        odd = flags_ref[1] == 1
        for j in range(half):
            own, own_factor = mine_ref[j], factor_ref[j : j + 1]
            other, other_factor = get_message(got_ref, j)
            total = jnp.where(odd, own + own_factor * other, other + other_factor * own)
            put_message(send_ref, j, total, own_factor * other_factor)

    return pl.pallas_call(
        kernel,
        in_specs=[smem_spec] + [vmem_spec] * 3,
        out_specs=vmem_spec,
        out_shape=shape((half, size + EXTRA, size), BF16),
        compiler_params=params(4),
    )(flags, mine, factor, got)


def join_end(flags, got, mine, factor, neighbour):
    half, size, _ = mine.shape
    pairs = len(got) + 1

    def kernel(flags_ref, *refs):
        got_refs, refs = refs[: len(got)], refs[len(got) :]
        mine_ref, factor_ref, neighbour_ref, keep_ref, send_ref, held = refs
        odd = flags_ref[1] == 1
        pair = flags_ref[0] >> 1
        for k, one in enumerate(got_refs, 1):
            held[pair ^ k] = one[...]
        held[pair] = jnp.zeros(held.shape[1:], BF16)
        for j in range(half):
            state = jnp.zeros((size, size), F32)
            for k in range(pairs - 1):
                other, other_factor = get_message(held.at[k], j)
                state = jnp.where(k < pair, other + other_factor * state, state)
            other, other_factor = get_message(neighbour_ref, j)
            even_state = jnp.where(odd, other, mine_ref[j])
            even_factor = jnp.where(odd, other_factor, factor_ref[j : j + 1])
            for_odd = even_state + even_factor * state
            keep_ref[j] = jnp.where(odd, for_odd, state).astype(BF16)
            send_ref[j] = jnp.where(odd, state, for_odd).astype(BF16)

    return pl.pallas_call(
        kernel,
        in_specs=[smem_spec] + [vmem_spec] * (len(got) + 3),
        out_specs=[vmem_spec] * 2,
        out_shape=[shape((half, size, size), BF16)] * 2,
        scratch_shapes=[pltpu.VMEM((pairs, half, size + EXTRA, size), BF16)],
        compiler_params=params(12),
    )(flags, *got, mine, factor, neighbour)


def lightning(flags, lin_query, lin_key, lin_value, log_decay, lin_gain, near, far):
    length, heads = log_decay.shape
    size = lin_key.shape[1] // heads
    half = heads // 2
    scale = 1.0 / math.sqrt(size)

    def kernel(flags_ref, query_ref, key_ref, value_ref, decay_ref, gain_ref, near_ref, far_ref,
               out_ref):
        down, across = sums_of(decay_ref)
        step = pl.program_id(0)
        second = (flags_ref[1] ^ step) == 1
        down = jnp.where(second, down[:, half:], down[:, :half])
        across = jnp.where(second, across[half:], across[:half])
        risen = jnp.exp(down) * scale
        row = lax.broadcasted_iota(jnp.int32, (length, length), 0)
        column = lax.broadcasted_iota(jnp.int32, (length, length), 1)
        causal = column <= row
        for j in range(half):
            at = slice(j * size, (j + 1) * size)
            query, key, value = query_ref[:, at], key_ref[:, at], value_ref[:, at]
            scores = lax.dot_general(
                query, key, (((1,), (1,)), ((), ())), preferred_element_type=F32
            )
            spread = down[:, j : j + 1] - across[j : j + 1]
            decays = jnp.exp(jnp.where(causal, spread, MASKED))
            mixed = (scores * (decays * scale)).astype(BF16)
            prior = jnp.where(step == 0, near_ref[j], far_ref[j])
            combined = jnp.dot(mixed, value, preferred_element_type=F32)
            combined = combined + risen[:, j : j + 1] * jnp.dot(
                query, prior, preferred_element_type=F32
            )
            square = jnp.mean(combined * combined, axis=-1, keepdims=True) + 1e-06
            out_ref[:, at] = (combined * lax.rsqrt(square) * gain_ref[:, at]).astype(BF16)

    block = pl.BlockSpec((length, half * size), lambda i, p: (0, p[1] ^ i))
    gains = pl.BlockSpec((1, half * size), lambda i, p: (0, p[1] ^ i))
    full = lambda dims: pl.BlockSpec(dims, lambda i, p: (0,) * len(dims))
    return pl.pallas_call(
        kernel,
        grid_spec=pltpu.PrefetchScalarGridSpec(
            num_scalar_prefetch=1,
            grid=(2,),
            in_specs=[
                block, block, block, full((heads, length)), gains,
                full((half, size, size)), full((half, size, size)),
            ],
            out_specs=block,
        ),
        out_shape=shape(lin_query.shape, BF16),
        compiler_params=params(12),
        cost_estimate=cost(6 * heads * length * size * size, 8 * length * heads * size),
    )(flags, lin_query, lin_key, lin_value, log_decay.T, lin_gain.reshape(1, -1), near, far)


def softmax_layer(flags, which, soft_query, pieces, turn, groups, size, heads, so_far=None):
    length, _ = soft_query.shape
    total = sum(one.shape[0] for one in pieces)
    scale = math.log2(math.e) / math.sqrt(size)
    given = () if so_far is None else (so_far,)

    def kernel(flags_ref, query_ref, *refs):
        piece_refs = refs[: len(pieces)]
        out_ref, keys, values, bias = refs[len(pieces) + len(given) :]
        at = 0
        for one in piece_refs:
            count = one.shape[0]
            keys[at : at + count] = one[:, :size]
            values[at : at + count, :size] = one[:, size:]
            at += count
        values[:, size:] = jnp.ones((total, size), BF16)

        @pl.when(pl.program_id(0) == 0)
        def _():
            me = flags_ref[0]
            row = lax.broadcasted_iota(jnp.int32, (length, length), 0)
            column = lax.broadcasted_iota(jnp.int32, (length, length), 1)
            ahead = column - row
            for k in range(total // length):
                source = me ^ (k ^ turn)
                late = ahead + (source - me) * length > 0
                bias[:, k * length : (k + 1) * length] = jnp.where(late, MASKED, 0.0)

        for h in range(heads):
            at = slice(h * size, (h + 1) * size)
            scores = lax.dot_general(
                query_ref[:, at], keys[...], (((1,), (1,)), ((), ())), preferred_element_type=F32
            )
            scores = scores * scale + bias[...]
            weights = jnp.exp2(scores - jnp.max(scores, axis=-1, keepdims=True))
            mixed = jnp.dot(weights.astype(BF16), values[...], preferred_element_type=F32)
            out_ref[:, at] = (mixed[:, :size] / mixed[:, size:]).astype(BF16)

    place = lambda g, f: (0, g if which is None else (f[1] ^ which) * groups + g)
    block = pl.BlockSpec((length, heads * size), place)
    return pl.pallas_call(
        kernel,
        grid_spec=pltpu.PrefetchScalarGridSpec(
            num_scalar_prefetch=1,
            grid=(groups,),
            in_specs=[block]
            + [pl.BlockSpec((one.shape[0], 2 * size), lambda g, f: (0, g)) for one in pieces]
            + [any_spec] * len(given),
            out_specs=block,
            scratch_shapes=[
                pltpu.VMEM((total, size), BF16),
                pltpu.VMEM((total, 2 * size), BF16),
                pltpu.VMEM((length, total), F32),
            ],
        ),
        out_shape=shape(soft_query.shape, BF16),
        input_output_aliases={2 + len(pieces): 0} if given else {},
        compiler_params=params(12),
        cost_estimate=cost(
            4 * groups * heads * size * length * total, 4 * length * groups * heads * size
        ),
    )(flags, soft_query, *pieces, *given)


def on_device(
    lin_query, lin_key, lin_value, log_decay, lin_gain,
    moe_input, routes, route_weight, gate_weight, up_weight, down_weight,
    soft_query, soft_kv,
):
    count, planes = lax.axis_size("ctx"), lax.axis_size("exp")
    me = lax.axis_index("ctx").astype(jnp.int32)
    flags = jnp.stack([me, me & 1, lax.axis_index("exp").astype(jnp.int32)])
    chips = range(2, count, 2)
    experts = gate_weight.shape[0] * planes
    groups, size = soft_kv.shape[1], soft_kv.shape[3]
    heads = soft_query.shape[1] // size // groups
    split = groups % 2 == 0
    kv_width = groups * 2 * size
    after = lambda value: tie(flags, value)[0]

    outgoing = pack(flags, moe_input, routes, planes, experts)
    soft_kv = tie(soft_kv, outgoing[0])[0]
    held = soft_kv.reshape(soft_kv.shape[0], kv_width)
    kv_other = held
    if split:
        odd = flags[1] == 1
        first, second = held[:, : kv_width // 2], held[:, kv_width // 2 :]
        held, kv_other = jnp.where(odd, second, first), jnp.where(odd, first, second)
    arrived = [outgoing[0]] + [swap(outgoing[p], "exp", p) for p in range(1, planes)]
    held = jnp.concatenate([held, swap(kv_other, "ctx", 1)])
    kv_got = [swap(held, "ctx", j) for j in chips]
    gate_first = fetch_gate(after(held), gate_weight)
    *arrived, held, gate_first = tie(*arrived, held, gate_first)

    own, other = arrange(arrived)
    rows = jnp.concatenate([own, swap(other, "ctx", 1)])
    got = [swap(rows, "ctx", j) for j in chips]
    mine, factor, message, other_gate, *own_rest = local_states(after(rows), lin_key, lin_value, log_decay, gate_weight)
    *got, message = tie(*got, message)
    near = jnp.concatenate([rows, *got])
    far = swap(near, "ctx", 1)
    neighbour = swap(message, "ctx", 1)

    sums = gate_and_up(flags, 0, near, [gate_first, *own_rest], up_weight)
    message = join_pair(after(sums[0]), mine, factor, neighbour)
    far, message = tie(far, message)
    got_states = [swap(message, "ctx", j) for j in chips]
    inner, early = gate_and_up(
        flags, 1, far, [other_gate], up_weight, sums, down_weight
    )
    send, early = down(flags, 1, inner, early, down_weight)
    summed = swap(send, "ctx", 1)
    keep, = down(after(send), 0, inner, early, down_weight)

    keep, *sends = fold_pair(keep, summed, count // 2)
    got_sums = [swap(one, "ctx", j) for j, one in zip(chips, sends)]
    attention = functools.partial(softmax_layer, size=size, heads=heads)
    pieces = [held, *kv_got]
    if split:
        whole = jnp.concatenate(tie(keep, *pieces)[1:])
        kv_far = swap(whole, "ctx", 1)
        soft_out = attention(after(sends[0]), 0, soft_query, [whole], 0, groups // 2)
        soft_out = attention(
            after(soft_out), 1, soft_query, [kv_far], 1, groups // 2, so_far=soft_out
        )
    else:
        soft_out = attention(after(sends[0]), None, soft_query, pieces, 0, groups)
    *got_sums, soft_out = tie(*got_sums, soft_out)
    own, send = fold_all(keep, got_sums)
    other = swap(send, "ctx", 1)
    state_near, state_send = join_end(after(send), got_states, mine, factor, neighbour)
    state_far = swap(state_send, "ctx", 1)
    result = finish(own, other, planes)
    returned = [result[0]] + [swap(result[p], "exp", p) for p in range(1, planes)]
    lin_out = lightning(
        after(result[0]), lin_query, lin_key, lin_value, log_decay, lin_gain,
        state_near, state_far,
    )
    *returned, lin_out = tie(*returned, lin_out)
    moe_out = unpack(flags, returned, routes, route_weight)
    return (lin_out, moe_out, soft_out)


def solution(mesh):
    placed = (
        P("ctx", "exp"),
        P("ctx", "exp"),
        P("ctx", "exp"),
        P("ctx", "exp"),
        P("exp"),
        P(("ctx", "exp"), None),
        P(("ctx", "exp"), None),
        P(("ctx", "exp"), None),
        P("exp", None, "ctx"),
        P("exp", None, "ctx"),
        P("exp", "ctx", None),
        P("ctx", "exp"),
        P("ctx", "exp", None, None),
    )

    return jax.shard_map(
        on_device,
        mesh=mesh,
        in_specs=placed,
        out_specs=(P("ctx", "exp"), P(("ctx", "exp"), None), P("ctx", "exp")),
        check_vma=False,
    )
```
